32 devices in a mesh: groups: 2 (over y), tok: 8 (over z, core), head: 2 (over x), tile: 1.
Axes of the slice: x: 2, y: 2, z: 4, core: 2. Of those that a mesh axis runs over, the one named last changes fastest.
Arguments:
- queries: bfloat16 [3072, 1, 16, 320], P(('groups', 'tok'), 'tile', 'head'), parts along dimension 0, may hold values from -6 to 6
- keys: bfloat16 [3072, 1, 16, 320], P(('groups', 'tok'), 'tile', 'head'), parts along dimension 0, may hold values from -6 to 6
- values: bfloat16 [3072, 1, 16, 320], P(('groups', 'tok'), 'tile', 'head'), parts along dimension 0, may hold values from -6 to 6
- rates: float32 [1, 16, 3072], P('tile', 'head', ('groups', 'tok')), parts along dimension 2, may hold values from 0.0003 to 0.003
- fast_weights: bfloat16 [1, 16, 3, 320, 320], P('tile', 'head'), may hold values from -0.3125 to 0.3125
- norm_gain: float32 [1, 16, 320], P('tile', 'head'), may hold values from 0.5 to 1.5
- frame_order: int32 [16], P('groups'), parts along dimension 0, may hold values from 0 to 7, each once
- gate_input: bfloat16 [24, 16, 8, 5120], P(None, ('groups', 'head'), 'tok', 'tile'), parts along dimension 1, may hold values from -6 to 6
- conv_weights: float32 [3, 3, 5120], P(None, None, 'tile'), may hold values from -2.5 to 2.5
Outputs:
- output: bfloat16 [24, 16, 8, 5120], P(None, ('groups', 'head'), 'tok', 'tile'), parts along dimension 1
The draws below stay inside these ranges and needn't reach their ends.
There are 2 independent parts, one for each index of `groups`. The reference program is written for one: setup_inputs(seed, part) draws one part's arguments, and reference() takes and returns one part's arrays. A program takes and returns all parts, laid end to end along the dimension named above; an argument that names none is the same for every part. Nothing has to cross between parts.
Inputs may be any that keep to these rules, and one draw needn't show every extreme that they name: frame_order names each of the 8 frames once.
All inputs are finite; a program needn't handle non-finite values.
Results may differ from the reference program's by a relative error of at most 0.011.
Values may be sent and summed in bfloat16 or wider, within the bound.
A program may use at most 64 MiB of HBM per device.

```python
import math
import jax
import jax.numpy as jnp
from jax import lax

HEADS = 16
DH = 320
FH = 320
HT = 24
D = 5120
HEAD_BLOCKS = 1
TILE_HEADS = 16
WT = 8
F = 8
TOKENS = 1536


def level_of(stream_key, extent, cuts, low, top_value):
    def one(dim, blocks):
        heights = jax.random.uniform(jax.random.fold_in(jax.random.fold_in(stream_key, 6), dim), (blocks,), jnp.float32, low / len(cuts), top_value / len(cuts))
        return jnp.repeat(jnp.exp(heights), extent[dim] // blocks).reshape((-1,) + (1,) * (len(extent) - dim - 1))

    level = one(*cuts[0])
    for cut in cuts[1:]:
        level = level * one(*cut)
    return level


def centred(stream_key, dims, scale, reach, pieces=(), kind=jnp.bfloat16):
    entries = scale * jax.random.normal(stream_key, dims, jnp.float32)
    if pieces:
        entries = entries * level_of(stream_key, dims, pieces, -0.22, 0.18)
    return jnp.clip(entries, -reach, reach).astype(kind)


def setup_inputs(seed: int = 0, part: int = 0) -> dict:
    streams_of = jax.random.split(jax.random.key(seed), 10)
    part_keys = jax.random.split(jax.random.fold_in(streams_of[9], part), 10)
    queries = centred(part_keys[0], (TOKENS, HEAD_BLOCKS, TILE_HEADS, DH), 1.0, 6.0, ((0, 8), (2, 2)))
    keys = centred(part_keys[1], (TOKENS, HEAD_BLOCKS, TILE_HEADS, DH), 1.0, 6.0, ((0, 8), (2, 2)))
    values = centred(part_keys[2], (TOKENS, HEAD_BLOCKS, TILE_HEADS, DH), 1.0, 6.0, ((0, 8), (2, 2)))
    rates = jnp.clip(jnp.exp(math.log(0.003) - 2.3025851 * jax.random.uniform(part_keys[3], (HEAD_BLOCKS, TILE_HEADS, TOKENS), jnp.float32) ** level_of(part_keys[3], (HEAD_BLOCKS, TILE_HEADS, TOKENS), ((1, 2), (2, 8)), -0.2, 0.2)), 0.0003, 0.003)
    fast_weights = centred(streams_of[4], (HEAD_BLOCKS, TILE_HEADS, 3, FH, DH), DH ** -0.5, 0.3125, ((1, 2),))
    norm_gain = jnp.clip(1.0 + 0.1 * jax.random.normal(streams_of[5], (HEAD_BLOCKS, TILE_HEADS, DH), jnp.float32), 0.5, 1.5)
    frame_order = jax.random.permutation(part_keys[6], F).astype(jnp.int32)
    gate_input = centred(part_keys[7], (HT, F, WT, D), 1.0, 6.0, ((1, 2), (2, 8)))
    conv_weights = centred(streams_of[8], (3, 3, D), 0.35, 2.5, (), jnp.float32)
    return {"queries": queries, "keys": keys, "values": values, "rates": rates, "fast_weights": fast_weights, "norm_gain": norm_gain, "frame_order": frame_order, "gate_input": gate_input, "conv_weights": conv_weights}


epsilon = 1e-06

def renormed(previous, gradient):
    before = previous.astype(jnp.float32)
    updated = before - gradient
    scale_old = jnp.sqrt(lax.optimization_barrier(jnp.mean(before * before, axis=-1, keepdims=True)) + epsilon)
    scale_new = jnp.sqrt(lax.optimization_barrier(jnp.mean(updated * updated, axis=-1, keepdims=True)) + epsilon)
    return (updated * (scale_old / scale_new)).astype(jnp.bfloat16)

def one_head(items):
    key_head, value_head, query_head, rate_head, weight_head, gain_head = items
    first_pre = jnp.dot(key_head, weight_head[0].T, preferred_element_type=jnp.float32)
    third_pre = jnp.dot(key_head, weight_head[1].T, preferred_element_type=jnp.float32)
    sigmoid_first = jax.nn.sigmoid(first_pre)
    activated = first_pre * sigmoid_first
    hidden = (activated * third_pre).astype(jnp.bfloat16)
    target = (-rate_head[:, None] * value_head.astype(jnp.float32)).astype(jnp.bfloat16)
    grad_down = jnp.dot(target.T, hidden, preferred_element_type=jnp.float32)
    hidden_grad = jnp.dot(target, weight_head[2], preferred_element_type=jnp.float32)
    grad_first_in = (hidden_grad * third_pre * sigmoid_first * (1.0 + first_pre * (1.0 - sigmoid_first))).astype(jnp.bfloat16)
    grad_third_in = (hidden_grad * activated).astype(jnp.bfloat16)
    grad_first = jnp.dot(grad_first_in.T, key_head, preferred_element_type=jnp.float32)
    grad_third = jnp.dot(grad_third_in.T, key_head, preferred_element_type=jnp.float32)
    gradients = jnp.stack([grad_first, grad_third, grad_down], axis=0)
    updated = renormed(weight_head, gradients)
    proj_first = jnp.dot(query_head, updated[0].T, preferred_element_type=jnp.float32)
    proj_third = jnp.dot(query_head, updated[1].T, preferred_element_type=jnp.float32)
    mixed_hidden = (jax.nn.silu(proj_first) * proj_third).astype(jnp.bfloat16)
    outputs = jnp.dot(mixed_hidden, updated[2].T, preferred_element_type=jnp.float32)
    normed = outputs * lax.rsqrt(lax.optimization_barrier(jnp.mean(outputs * outputs, axis=-1, keepdims=True)) + epsilon) * gain_head[None, :]
    return normed.astype(jnp.bfloat16)

def reference(queries, keys, values, rates, fast_weights, norm_gain, frame_order, gate_input, conv_weights):
    query_rows = jnp.moveaxis(queries.reshape(TOKENS, HEADS, DH), 1, 0)
    key_rows = jnp.moveaxis(keys.reshape(TOKENS, HEADS, DH), 1, 0)
    value_rows = jnp.moveaxis(values.reshape(TOKENS, HEADS, DH), 1, 0)
    token_rates = rates.reshape(HEADS, TOKENS)
    weights = fast_weights.reshape(HEADS, 3, DH, DH)
    head_gains = norm_gain.reshape(HEADS, DH)
    normed_all = lax.map(one_head, (key_rows, value_rows, query_rows, token_rates, weights, head_gains))
    flat = jnp.moveaxis(normed_all, 0, 1).reshape(F, HT, WT, D)
    numbers = jnp.arange(F, dtype=jnp.int32)
    inverse = lax.optimization_barrier(jnp.sum(jnp.where(frame_order[None, :] == numbers[:, None], numbers[None, :], 0), axis=1)).astype(jnp.int32)
    frames = jnp.take(flat, inverse, axis=0)
    frame_grid = jnp.transpose(frames, (1, 0, 2, 3))
    padded = jnp.pad(frame_grid, ((1, 1), (0, 0), (1, 1), (0, 0)))
    result = jnp.zeros((HT, F, WT, D), jnp.float32)
    for row_tap in range(3):
        for col_tap in range(3):
            result = result + conv_weights[row_tap, col_tap] * padded[row_tap:row_tap + HT, :, col_tap:col_tap + WT].astype(jnp.float32)
    rounded = lax.optimization_barrier(result.astype(jnp.bfloat16))
    return (rounded.astype(jnp.float32) * jax.nn.silu(gate_input.astype(jnp.float32))).astype(jnp.bfloat16)
```

```python
import functools

import jax
import jax.numpy as jnp
from jax import lax
from jax.experimental import pallas as pl
from jax.experimental.pallas import tpu as pltpu
from jax.sharding import PartitionSpec as P

MESH = pl.DeviceIdType.MESH

epsilon = 1e-06


def renormed(previous, gradient):
    before = previous.astype(jnp.float32)
    updated = before - gradient
    scale_old = jnp.sqrt(jnp.mean(before * before, axis=-1, keepdims=True) + epsilon)
    scale_new = jnp.sqrt(jnp.mean(updated * updated, axis=-1, keepdims=True) + epsilon)
    return (updated * (scale_old / scale_new)).astype(jnp.bfloat16)


def split_rows(
    queries, keys, values, rates, fast_weights, norm_gain, frame_order, gate_input, conv_weights
):
    tok_rows = queries.shape[0]
    head_count = queries.shape[1] * queries.shape[2]
    head_size = queries.shape[3]
    query_rows = queries.reshape(tok_rows, head_count, head_size)
    key_rows = keys.reshape(tok_rows, head_count, head_size)
    value_rows = values.reshape(tok_rows, head_count, head_size)
    token_rates = rates.reshape(head_count, tok_rows)
    weights = fast_weights.reshape(head_count, 3, head_size, head_size)
    head_gains = norm_gain.reshape(head_count, head_size)
    first_pre = jnp.einsum(
        "thd,hfd->htf", key_rows, weights[:, 0], preferred_element_type=jnp.float32
    )
    third_pre = jnp.einsum(
        "thd,hfd->htf", key_rows, weights[:, 1], preferred_element_type=jnp.float32
    )
    sigmoid_first = jax.nn.sigmoid(first_pre)
    activated = first_pre * sigmoid_first
    hidden = (activated * third_pre).astype(jnp.bfloat16)
    target = (-token_rates.T[:, :, None] * value_rows.astype(jnp.float32)).astype(jnp.bfloat16)
    grad_down = jnp.einsum("thd,htf->hdf", target, hidden, preferred_element_type=jnp.float32)
    hidden_grad = jnp.einsum(
        "thd,hdf->htf", target, weights[:, 2], preferred_element_type=jnp.float32
    )
    grad_first_in = (
        hidden_grad * third_pre * sigmoid_first * (1.0 + first_pre * (1.0 - sigmoid_first))
    ).astype(jnp.bfloat16)
    grad_third_in = (hidden_grad * activated).astype(jnp.bfloat16)
    grad_first = jnp.einsum(
        "htf,thd->hfd", grad_first_in, key_rows, preferred_element_type=jnp.float32
    )
    grad_third = jnp.einsum(
        "htf,thd->hfd", grad_third_in, key_rows, preferred_element_type=jnp.float32
    )
    gradients = jnp.stack([grad_first, grad_third, grad_down], axis=1)
    row_share = lax.psum_scatter(gradients, "tok", scatter_dimension=2, tiled=True)
    row_count = row_share.shape[2]
    own_rows = lax.dynamic_slice_in_dim(weights, lax.axis_index("tok") * row_count, row_count, 2)
    updated = lax.all_gather(renormed(own_rows, row_share), "tok", axis=2, tiled=True)
    proj_first = jnp.einsum(
        "thd,hfd->thf", query_rows, updated[:, 0], preferred_element_type=jnp.float32
    )
    proj_third = jnp.einsum(
        "thd,hfd->thf", query_rows, updated[:, 1], preferred_element_type=jnp.float32
    )
    mixed_hidden = (jax.nn.silu(proj_first) * proj_third).astype(jnp.bfloat16)
    outputs = jnp.einsum(
        "thf,hdf->thd", mixed_hidden, updated[:, 2], preferred_element_type=jnp.float32
    )
    normed = (
        outputs
        * lax.rsqrt(jnp.mean(outputs * outputs, axis=-1, keepdims=True) + epsilon)
        * head_gains[None]
    )
    normed = normed.astype(jnp.bfloat16)
    height = gate_input.shape[0]
    col_width = gate_input.shape[2]
    shards = lax.axis_size("tok")
    full_width = col_width * shards
    channels_here = head_count * head_size
    frame_grid = normed.reshape(height, full_width, channels_here)
    own_taps = lax.dynamic_slice_in_dim(
        conv_weights, lax.axis_index("head") * channels_here, channels_here, 2
    )
    padded = jnp.pad(frame_grid, ((1, 1), (1, 1), (0, 0)))
    local_sum = jnp.zeros((height, full_width, channels_here), jnp.float32)
    for row_tap in range(3):
        for col_tap in range(3):
            local_sum = local_sum + own_taps[row_tap, col_tap] * padded[
                row_tap : row_tap + height, col_tap : col_tap + full_width
            ].astype(jnp.float32)
    outgoing = local_sum.astype(jnp.bfloat16).reshape(height, shards, col_width, channels_here)
    arrived = lax.all_to_all(outgoing, "tok", split_axis=1, concat_axis=1, tiled=True)
    frame_count = frame_order.shape[0]
    numbers = jnp.arange(frame_count, dtype=jnp.int32)
    inverse = jnp.sum(
        jnp.where(frame_order[None, :] == numbers[:, None], numbers[None, :], 0), axis=1
    )
    ordered = jnp.take(arrived, inverse, axis=1)
    tile_block = lax.all_to_all(ordered, "head", split_axis=1, concat_axis=3, tiled=True)
    return (tile_block.astype(jnp.float32) * jax.nn.silu(gate_input.astype(jnp.float32))).astype(
        jnp.bfloat16
    )


def dot_nt(left, right):
    return lax.dot_general(left, right, (((1,), (1,)), ((), ())), preferred_element_type=jnp.float32)


def dot_nn(left, right):
    return lax.dot_general(left, right, (((1,), (0,)), ((), ())), preferred_element_type=jnp.float32)


def dot_tn(left, right):
    return lax.dot_general(left, right, (((0,), (0,)), ((), ())), preferred_element_type=jnp.float32)


def head_kernel(
    shards, head_shards, width,
    order_ref, query_rows_ref, key_rows_ref, value_rows_ref, rates_ref, weights_ref, gains_ref, taps_ref, conv_ref,
    pairs_ref, queries_ref, pairs_in, queries_in, weights_in, sums, sums_out, sums_in, renewed, mixed_rows, frame_pair, outgoing, arrived_ref,
    inverse_ref,
    pair_send, pair_recv, query_send, query_recv, sum_send, sum_recv, out_send, out_recv, own_sem, own_out_sem,
):
    tok = lax.axis_index("tok")
    head = lax.axis_index("head")
    mates = shards // 2
    near_count = mates // 2
    half, seat = tok // mates, tok % mates
    other = 1 - half
    size = weights_ref.shape[-1]
    rows = key_rows_ref.shape[1]
    everyone = shards * head_shards
    pair_steps = outgoing.shape[1]
    lane_groups = frame_pair.shape[0]

    own_copies = [
        pltpu.make_async_copy(weights_ref.at[other * mates + seat], weights_in.at[0], own_sem.at[0]),
        pltpu.make_async_copy(weights_ref.at[half * mates + seat], weights_in.at[1], own_sem.at[1]),
    ]
    for copy in own_copies:
        copy.start()

    barrier = pltpu.get_barrier_semaphore()

    def greet(step, carry):
        index = (head * shards + tok + step) % everyone
        pl.semaphore_signal(
            barrier, inc=1, device_id={"head": index // shards, "tok": index % shards}, device_id_type=MESH
        )
        return carry

    lax.fori_loop(1, everyone, greet, 0)
    frame_count = order_ref.shape[0]
    for number in range(frame_count):
        place = jnp.int32(0)
        for shard in range(frame_count):
            place = jnp.where(order_ref[shard] == number, jnp.int32(shard), place)
        inverse_ref[number] = place

    token_rates = -rates_ref[...].T
    lane = lax.broadcasted_iota(jnp.int32, token_rates.shape, 1)

    def pack_query(index, carry):
        block = query_rows_ref[index]
        queries_ref[index] = jnp.concatenate([block[: rows // 2], block[rows // 2 :]], axis=1)
        return carry

    def pack_pair(step, carry):
        index = (other * mates + step) % shards
        rate = jnp.sum(jnp.where(lane == index, token_rates, 0.0), axis=1, keepdims=True)
        target = (rate * value_rows_ref[index].astype(jnp.float32)).astype(jnp.bfloat16)
        pairs_ref[index] = jnp.concatenate([key_rows_ref[index], target], axis=1)
        return carry

    lax.fori_loop(0, mates, pack_pair, 0)
    lax.fori_loop(0, shards, pack_query, 0)
    pl.semaphore_wait(barrier, everyone - 1)

    def mate_at(step):
        return (seat // 2 + step // 2) % near_count * 2 + (seat + step) % 2

    def mate_from(step):
        return (seat // 2 - step // 2 + near_count) % near_count * 2 + (seat + step) % 2

    def pair_copy(slot, to, at):
        chosen = other if slot == 0 else half
        return pltpu.make_async_remote_copy(
            src_ref=pairs_ref.at[chosen * mates + to],
            dst_ref=pairs_in.at[slot, at],
            send_sem=pair_send.at[slot, to],
            recv_sem=pair_recv.at[slot, at],
            device_id={"tok": half * mates + to},
            device_id_type=MESH,
        )

    def query_copy(to, at):
        return pltpu.make_async_remote_copy(
            src_ref=queries_ref.at[to],
            dst_ref=queries_in.at[at],
            send_sem=query_send.at[to],
            recv_sem=query_recv.at[at],
            device_id={"tok": to},
            device_id_type=MESH,
        )

    def out_copy(to_head, to_tok, step, from_head, from_tok):
        return pltpu.make_async_remote_copy(
            src_ref=outgoing.at[to_head, step, to_tok],
            dst_ref=arrived_ref.at[from_head, from_tok, step],
            send_sem=out_send.at[to_head, step, to_tok],
            recv_sem=out_recv.at[from_head, step, from_tok],
            device_id={"head": to_head, "tok": to_tok},
            device_id_type=MESH,
        )

    def sum_copy(part):
        return pltpu.make_async_remote_copy(
            src_ref=sums_out.at[part],
            dst_ref=sums_in.at[part],
            send_sem=sum_send.at[part],
            recv_sem=sum_recv.at[part],
            device_id={"tok": other * mates + seat},
            device_id_type=MESH,
        )

    def each_mate(core, send):
        def to_chip(step, carry):
            to = (seat // 2 + step) % near_count * 2 + core

            @pl.when(to != seat)
            def _():
                send(to)

            return carry

        lax.fori_loop(0, near_count, to_chip, 0)

    def send_pairs(slot, core):
        each_mate(core, lambda to: pair_copy(slot, to, seat).start())

    def send_queries_home(core):
        each_mate(core, lambda to: query_copy(half * mates + to, tok).start())

    def send_queries_across(core):
        def to_chip(step, carry):
            chip = other * step + half * (near_count - 1 - step)
            query_copy(other * mates + chip * 2 + core, tok).start()
            return carry

        lax.fori_loop(0, near_count, to_chip, 0)

    goes_first = seat % 2 == 0

    send_pairs(0, 0)
    send_queries_across(0)
    send_pairs(0, 1)

    lax.fori_loop(mates, shards, pack_pair, 0)

    send_pairs(1, 0)

    @pl.when(jnp.logical_not(goes_first))
    def _():
        send_queries_home(0)
        send_queries_across(1)


    block_copies = [
        pltpu.make_async_copy(pairs_ref.at[other * mates + seat], pairs_in.at[0, seat], own_sem.at[2]),
        pltpu.make_async_copy(pairs_ref.at[half * mates + seat], pairs_in.at[1, seat], own_sem.at[3]),
        pltpu.make_async_copy(queries_ref.at[tok], queries_in.at[tok], own_sem.at[4]),
    ]
    for copy in block_copies:
        copy.start()
    for copy in own_copies + block_copies:
        copy.wait()

    for slot in range(2):
        sums[...] = jnp.zeros_like(sums)

        def gather_block(step, carry):
            source = mate_from(step)

            @pl.when(step > 0)
            def _():
                pair_copy(slot, seat, source).wait_recv()

            block = pairs_in[slot, source]
            key_rows, target = block[:, :size], block[:, size:]
            first_pre = dot_nt(key_rows, weights_in[slot, 0])
            third_pre = dot_nt(key_rows, weights_in[slot, 1])
            hidden_grad = dot_nn(target, weights_in[slot, 2])
            sigmoid_first = jax.nn.sigmoid(first_pre)
            activated = first_pre * sigmoid_first
            hidden = (activated * third_pre).astype(jnp.bfloat16)
            grad_first_in = (
                hidden_grad * third_pre * sigmoid_first * (1.0 + first_pre * (1.0 - sigmoid_first))
            ).astype(jnp.bfloat16)
            grad_third_in = (hidden_grad * activated).astype(jnp.bfloat16)
            sums[0] += dot_tn(grad_first_in, key_rows)
            sums[1] += dot_tn(grad_third_in, key_rows)
            sums[2] += dot_tn(target, hidden)
            return carry

        lax.fori_loop(0, mates, gather_block, 0)
        if slot == 0:
            for part in range(3):
                total = sums[part].astype(jnp.bfloat16)
                sums_out[part] = jnp.concatenate([total[: size // 2], total[size // 2 :]], axis=1)
            sum_copy(0).start()
            sum_copy(1).start()
            sum_copy(2).start()

            @pl.when(goes_first)
            def _():
                send_queries_home(0)
                send_queries_across(1)
                send_pairs(1, 1)
                send_queries_home(1)


            @pl.when(jnp.logical_not(goes_first))
            def _():
                send_pairs(1, 1)
                send_queries_home(1)


    def renew(part):
        sum_copy(part).wait_recv()
        packed = sums_in[part].astype(jnp.float32)
        total = sums[part] + jnp.concatenate([packed[:, :size], packed[:, size:]], axis=0)
        renewed[part] = renormed(weights_in[1, part], total)

    renew(0)
    renew(1)

    def mix_query(step, carry):
        source = (half + step // mates) % 2 * mates + mate_from(step % mates)

        @pl.when(step > 0)
        def _():
            query_copy(tok, source).wait_recv()

        packed = queries_in[source]
        query_rows = jnp.concatenate([packed[:, :size], packed[:, size:]], axis=0)
        proj_first = dot_nt(query_rows, renewed[0])
        proj_third = dot_nt(query_rows, renewed[1])
        mixed_rows[source] = (proj_first * jax.nn.sigmoid(proj_first) * proj_third).astype(jnp.bfloat16)
        return carry

    lax.fori_loop(0, shards, mix_query, 0)
    renew(2)

    column = lax.broadcasted_iota(jnp.int32, (rows, size), 0) % width
    gain = gains_ref[pl.ds(tok, 1), :]
    height = rows // width
    edge = jnp.zeros((width, size), jnp.float32)

    def two_frames(first, second):
        mixed = jnp.concatenate([mixed_rows[first], mixed_rows[second]], axis=0)
        outputs = dot_nt(mixed, renewed[2])
        normed = outputs * lax.rsqrt(jnp.mean(outputs * outputs, axis=-1, keepdims=True) + epsilon) * gain
        normed = normed.astype(jnp.bfloat16).astype(jnp.float32)
        return jnp.concatenate([one_frame(normed[:rows]), one_frame(normed[rows:])], axis=1)

    def one_frame(middle):
        left = jnp.where(column == 0, 0.0, pltpu.roll(middle, 1, 0))
        right = jnp.where(column == width - 1, 0.0, pltpu.roll(middle, rows - 1, 0))
        bands = [
            taps_ref[3 * tap : 3 * tap + 1, :] * left
            + taps_ref[3 * tap + 1 : 3 * tap + 2, :] * middle
            + taps_ref[3 * tap + 2 : 3 * tap + 3, :] * right
            for tap in range(3)
        ]
        above = jnp.concatenate([edge, bands[0][:-width]], axis=0)
        below = jnp.concatenate([bands[2][width:], edge], axis=0)
        return above + bands[1] + below

    def frame_step(index, carry):
        to_head = (head + 1 + index // pair_steps) % head_shards
        step = index % pair_steps
        number = (to_head * pair_steps + step) * 2
        both = two_frames(inverse_ref[number], inverse_ref[number + 1])
        for lane in range(lane_groups):
            frame_pair[lane] = both[:, lane * 128 : (lane + 1) * 128]
        for x in range(width):
            for lane in range(lane_groups):
                outgoing[to_head, step, x, :, lane * 128 : (lane + 1) * 128] = frame_pair[
                    lane, pl.ds(x, height, stride=width), :
                ].astype(jnp.bfloat16)

        def send_out(offset, inner):
            to_tok = (tok + offset) % shards
            at_home = jnp.logical_and(to_head == head, offset == 0)

            @pl.when(at_home)
            def _():
                pltpu.make_async_copy(
                    outgoing.at[head, step, tok], arrived_ref.at[head, tok, step], own_out_sem.at[step]
                ).start()

            @pl.when(jnp.logical_not(at_home))
            def _():
                out_copy(to_head, to_tok, step, head, tok).start()

            return inner

        lax.fori_loop(0, shards, send_out, 0)
        return carry

    lax.fori_loop(0, head_shards * pair_steps, frame_step, 0)

    for step in range(pair_steps):
        pltpu.make_async_copy(
            outgoing.at[head, step, tok], arrived_ref.at[head, tok, step], own_out_sem.at[step]
        ).wait()

    def take_step(index, carry):
        from_head = (head + 1 + index // pair_steps) % head_shards
        step = index % pair_steps

        def take_out(offset, inner):
            from_tok = (tok - offset + shards) % shards

            @pl.when(jnp.logical_not(jnp.logical_and(from_head == head, offset == 0)))
            def _():
                out_copy(head, tok, step, from_head, from_tok).wait_recv()

            return inner

        lax.fori_loop(0, shards, take_out, 0)
        for pair in range(shards // 2):
            even = arrived_ref[from_head, 2 * pair, step]
            odd = arrived_ref[from_head, 2 * pair + 1, step]
            lanes = pl.ds(pl.multiple_of((from_head * shards + 2 * pair) * size, 2 * size), 2 * size)
            conv_ref[2 * step, :, lanes] = jnp.concatenate([even[:, :size], odd[:, :size]], axis=1)
            conv_ref[2 * step + 1, :, lanes] = jnp.concatenate([even[:, size:], odd[:, size:]], axis=1)
        return carry

    lax.fori_loop(0, head_shards * pair_steps, take_step, 0)

    for slot in range(2):
        def sent_pair(step, carry):
            pair_copy(slot, mate_at(step), seat).wait_send()
            return carry

        lax.fori_loop(1, mates, sent_pair, 0)

    def sent_query(step, carry):
        query_copy((tok + step) % shards, tok).wait_send()
        return carry

    lax.fori_loop(1, shards, sent_query, 0)
    for part in range(3):
        sum_copy(part).wait_send()
    for step in range(pair_steps):
        def sent_out(offset, carry):
            index = (head * shards + tok + offset) % everyone
            out_copy(index // shards, index % shards, step, head, tok).wait_send()
            return carry

        lax.fori_loop(1, everyone, sent_out, 0)


def by_heads(
    queries, keys, values, rates, fast_weights, norm_gain, frame_order, gate_input, conv_weights
):
    rows = queries.shape[0]
    heads = queries.shape[1] * queries.shape[2]
    size = queries.shape[3]
    shards = lax.axis_size("tok")
    head_shards = lax.axis_size("head")
    height = gate_input.shape[0]
    frames_here = gate_input.shape[1]
    pair_steps = frames_here // 2
    width = rows // height

    def by_head(values_here):
        return values_here.reshape(rows, heads, size).transpose(1, 0, 2)

    own_channel = (lax.axis_index("head") * heads + lax.axis_index("tok")) * size
    taps = lax.dynamic_slice_in_dim(conv_weights, own_channel, size, 2).reshape(9, size)
    mates = shards // 2
    in_vmem = pl.BlockSpec(memory_space=pltpu.VMEM)
    anywhere = pl.BlockSpec(memory_space=pl.ANY)
    dma = pltpu.SemaphoreType.DMA
    conv = pl.pallas_call(
        functools.partial(head_kernel, shards, head_shards, width),
        out_shape=jax.ShapeDtypeStruct((frames_here, height, head_shards * shards * size), jnp.bfloat16),
        in_specs=[pl.BlockSpec(memory_space=pltpu.SMEM)] + [in_vmem] * 4 + [anywhere, in_vmem, in_vmem],
        out_specs=in_vmem,
        scratch_shapes=[
            pltpu.VMEM((heads, rows, 2 * size), jnp.bfloat16),
            pltpu.VMEM((heads, rows // 2, 2 * size), jnp.bfloat16),
            pltpu.VMEM((2, mates, rows, 2 * size), jnp.bfloat16),
            pltpu.VMEM((shards, rows // 2, 2 * size), jnp.bfloat16),
            pltpu.VMEM((2, 3, size, size), jnp.bfloat16),
            pltpu.VMEM((3, size, size), jnp.float32),
            pltpu.VMEM((3, size // 2, 2 * size), jnp.bfloat16),
            pltpu.VMEM((3, size // 2, 2 * size), jnp.bfloat16),
            pltpu.VMEM((3, size, size), jnp.bfloat16),
            pltpu.VMEM((shards, rows, size), jnp.bfloat16),
            pltpu.VMEM((2 * size // 128, rows, 128), jnp.float32),
            pltpu.VMEM((head_shards, pair_steps, shards, height, 2 * size), jnp.bfloat16),
            pltpu.VMEM((head_shards, shards, pair_steps, height, 2 * size), jnp.bfloat16),
            pltpu.SMEM((shards,), jnp.int32),
            dma((2, mates)),
            dma((2, mates)),
            dma((shards,)),
            dma((shards,)),
            dma((3,)),
            dma((3,)),
            dma((head_shards, pair_steps, shards)),
            dma((head_shards, pair_steps, shards)),
            dma((5,)),
            dma((pair_steps,)),
        ],
        compiler_params=pltpu.CompilerParams(
            collective_id=0, has_side_effects=True, vmem_limit_bytes=50 * 1024 * 1024
        ),
    )(
        frame_order,
        by_head(queries),
        by_head(keys),
        by_head(values),
        rates.reshape(heads, rows),
        fast_weights.reshape(heads, 3, size, size),
        norm_gain.reshape(heads, size),
        taps,
    )
    conv = conv.transpose(1, 0, 2).reshape(gate_input.shape)
    return (conv.astype(jnp.float32) * jax.nn.silu(gate_input.astype(jnp.float32))).astype(jnp.bfloat16)


def local(
    queries, keys, values, rates, fast_weights, norm_gain, frame_order, gate_input, conv_weights
):
    shards = lax.axis_size("tok")
    heads = queries.shape[1] * queries.shape[2]
    one_head_each = heads == shards and shards % 2 == 0
    one_column_each = gate_input.shape[2] == 1 and queries.shape[0] == gate_input.shape[0] * shards
    even = queries.shape[0] % 2 == 0 and gate_input.shape[1] % 2 == 0 and shards % 8 == 0
    even = even and 2 * queries.shape[3] % 128 == 0
    form = by_heads if one_head_each and one_column_each and even else split_rows
    return form(
        queries, keys, values, rates, fast_weights, norm_gain, frame_order, gate_input, conv_weights
    )


def solution(mesh):
    in_specs = (
        P(("groups", "tok"), "tile", "head", None),
        P(("groups", "tok"), "tile", "head", None),
        P(("groups", "tok"), "tile", "head", None),
        P("tile", "head", ("groups", "tok")),
        P("tile", "head", None, None, None),
        P("tile", "head", None),
        P("groups"),
        P(None, ("groups", "head"), "tok", "tile"),
        P(None, None, "tile"),
    )
    out_specs = P(None, ("groups", "head"), "tok", "tile")
    return jax.shard_map(local, mesh=mesh, in_specs=in_specs, out_specs=out_specs, check_vma=False)
```

```python
import functools

import jax
import jax.numpy as jnp
from jax import lax
from jax.experimental import pallas as pl
from jax.experimental.pallas import tpu as pltpu
from jax.sharding import PartitionSpec as P

MESH = pl.DeviceIdType.MESH

epsilon = 1e-06


def renormed(previous, gradient):
    before = previous.astype(jnp.float32)
    updated = before - gradient
    scale_old = jnp.sqrt(jnp.mean(before * before, axis=-1, keepdims=True) + epsilon)
    scale_new = jnp.sqrt(jnp.mean(updated * updated, axis=-1, keepdims=True) + epsilon)
    return (updated * (scale_old / scale_new)).astype(jnp.bfloat16)


def split_rows(
    queries, keys, values, rates, fast_weights, norm_gain, frame_order, gate_input, conv_weights
):
    tok_rows = queries.shape[0]
    head_count = queries.shape[1] * queries.shape[2]
    head_size = queries.shape[3]
    query_rows = queries.reshape(tok_rows, head_count, head_size)
    key_rows = keys.reshape(tok_rows, head_count, head_size)
    value_rows = values.reshape(tok_rows, head_count, head_size)
    token_rates = rates.reshape(head_count, tok_rows)
    weights = fast_weights.reshape(head_count, 3, head_size, head_size)
    head_gains = norm_gain.reshape(head_count, head_size)
    first_pre = jnp.einsum(
        "thd,hfd->htf", key_rows, weights[:, 0], preferred_element_type=jnp.float32
    )
    third_pre = jnp.einsum(
        "thd,hfd->htf", key_rows, weights[:, 1], preferred_element_type=jnp.float32
    )
    sigmoid_first = jax.nn.sigmoid(first_pre)
    activated = first_pre * sigmoid_first
    hidden = (activated * third_pre).astype(jnp.bfloat16)
    target = (-token_rates.T[:, :, None] * value_rows.astype(jnp.float32)).astype(jnp.bfloat16)
    grad_down = jnp.einsum("thd,htf->hdf", target, hidden, preferred_element_type=jnp.float32)
    hidden_grad = jnp.einsum(
        "thd,hdf->htf", target, weights[:, 2], preferred_element_type=jnp.float32
    )
    grad_first_in = (
        hidden_grad * third_pre * sigmoid_first * (1.0 + first_pre * (1.0 - sigmoid_first))
    ).astype(jnp.bfloat16)
    grad_third_in = (hidden_grad * activated).astype(jnp.bfloat16)
    grad_first = jnp.einsum(
        "htf,thd->hfd", grad_first_in, key_rows, preferred_element_type=jnp.float32
    )
    grad_third = jnp.einsum(
        "htf,thd->hfd", grad_third_in, key_rows, preferred_element_type=jnp.float32
    )
    gradients = jnp.stack([grad_first, grad_third, grad_down], axis=1)
    row_share = lax.psum_scatter(gradients, "tok", scatter_dimension=2, tiled=True)
    row_count = row_share.shape[2]
    own_rows = lax.dynamic_slice_in_dim(weights, lax.axis_index("tok") * row_count, row_count, 2)
    updated = lax.all_gather(renormed(own_rows, row_share), "tok", axis=2, tiled=True)
    proj_first = jnp.einsum(
        "thd,hfd->thf", query_rows, updated[:, 0], preferred_element_type=jnp.float32
    )
    proj_third = jnp.einsum(
        "thd,hfd->thf", query_rows, updated[:, 1], preferred_element_type=jnp.float32
    )
    mixed_hidden = (jax.nn.silu(proj_first) * proj_third).astype(jnp.bfloat16)
    outputs = jnp.einsum(
        "thf,hdf->thd", mixed_hidden, updated[:, 2], preferred_element_type=jnp.float32
    )
    normed = (
        outputs
        * lax.rsqrt(jnp.mean(outputs * outputs, axis=-1, keepdims=True) + epsilon)
        * head_gains[None]
    )
    normed = normed.astype(jnp.bfloat16)
    height = gate_input.shape[0]
    col_width = gate_input.shape[2]
    shards = lax.axis_size("tok")
    full_width = col_width * shards
    channels_here = head_count * head_size
    frame_grid = normed.reshape(height, full_width, channels_here)
    own_taps = lax.dynamic_slice_in_dim(
        conv_weights, lax.axis_index("head") * channels_here, channels_here, 2
    )
    padded = jnp.pad(frame_grid, ((1, 1), (1, 1), (0, 0)))
    local_sum = jnp.zeros((height, full_width, channels_here), jnp.float32)
    for row_tap in range(3):
        for col_tap in range(3):
            local_sum = local_sum + own_taps[row_tap, col_tap] * padded[
                row_tap : row_tap + height, col_tap : col_tap + full_width
            ].astype(jnp.float32)
    outgoing = local_sum.astype(jnp.bfloat16).reshape(height, shards, col_width, channels_here)
    arrived = lax.all_to_all(outgoing, "tok", split_axis=1, concat_axis=1, tiled=True)
    frame_count = frame_order.shape[0]
    numbers = jnp.arange(frame_count, dtype=jnp.int32)
    inverse = jnp.sum(
        jnp.where(frame_order[None, :] == numbers[:, None], numbers[None, :], 0), axis=1
    )
    ordered = jnp.take(arrived, inverse, axis=1)
    tile_block = lax.all_to_all(ordered, "head", split_axis=1, concat_axis=3, tiled=True)
    return (tile_block.astype(jnp.float32) * jax.nn.silu(gate_input.astype(jnp.float32))).astype(
        jnp.bfloat16
    )


def dot_nt(left, right):
    return lax.dot_general(left, right, (((1,), (1,)), ((), ())), preferred_element_type=jnp.float32)


def dot_nn(left, right):
    return lax.dot_general(left, right, (((1,), (0,)), ((), ())), preferred_element_type=jnp.float32)


def dot_tn(left, right):
    return lax.dot_general(left, right, (((0,), (0,)), ((), ())), preferred_element_type=jnp.float32)


def head_kernel(
    shards, head_shards, width,
    order_ref, query_rows_ref, key_rows_ref, value_rows_ref, rates_ref, weights_ref, gains_ref, taps_ref, gate_ref, gated_ref,
    gate_in, gate_rows, pairs_ref, queries_ref, pairs_in, queries_in, weights_in, sums, sums_out, sums_in, renewed, mixed_rows, frame_pair, outgoing, arrived_ref,
    inverse_ref,
    pair_send, pair_recv, query_send, query_recv, sum_send, sum_recv, out_send, out_recv, own_sem, own_out_sem,
):
    tok = lax.axis_index("tok")
    head = lax.axis_index("head")
    mates = shards // 2
    near_count = mates // 2
    half, seat = tok // mates, tok % mates
    other = 1 - half
    size = weights_ref.shape[-1]
    rows = key_rows_ref.shape[1]
    everyone = shards * head_shards
    pair_steps = outgoing.shape[1]
    lane_groups = frame_pair.shape[0]

    own_copies = [
        pltpu.make_async_copy(weights_ref.at[other * mates + seat], weights_in.at[0], own_sem.at[0]),
        pltpu.make_async_copy(weights_ref.at[half * mates + seat], weights_in.at[1], own_sem.at[1]),
    ]
    for copy in own_copies:
        copy.start()

    barrier = pltpu.get_barrier_semaphore()

    def greet(step, carry):
        index = (head * shards + tok + step) % everyone
        pl.semaphore_signal(
            barrier, inc=1, device_id={"head": index // shards, "tok": index % shards}, device_id_type=MESH
        )
        return carry

    lax.fori_loop(1, everyone, greet, 0)
    frame_count = order_ref.shape[0]
    for number in range(frame_count):
        place = jnp.int32(0)
        for shard in range(frame_count):
            place = jnp.where(order_ref[shard] == number, jnp.int32(shard), place)
        inverse_ref[number] = place

    token_rates = -rates_ref[...].T
    lane = lax.broadcasted_iota(jnp.int32, token_rates.shape, 1)

    def pack_query(index, carry):
        block = query_rows_ref[index]
        queries_ref[index] = jnp.concatenate([block[: rows // 2], block[rows // 2 :]], axis=1)
        return carry

    def pack_pair(step, carry):
        index = (other * mates + step) % shards
        rate = jnp.sum(jnp.where(lane == index, token_rates, 0.0), axis=1, keepdims=True)
        target = (rate * value_rows_ref[index].astype(jnp.float32)).astype(jnp.bfloat16)
        pairs_ref[index] = jnp.concatenate([key_rows_ref[index], target], axis=1)
        return carry

    lax.fori_loop(0, mates, pack_pair, 0)
    lax.fori_loop(0, shards, pack_query, 0)
    pl.semaphore_wait(barrier, everyone - 1)

    def mate_at(step):
        return (seat // 2 + step // 2) % near_count * 2 + (seat + step) % 2

    def mate_from(step):
        return (seat // 2 - step // 2 + near_count) % near_count * 2 + (seat + step) % 2

    def pair_copy(slot, to, at):
        chosen = other if slot == 0 else half
        return pltpu.make_async_remote_copy(
            src_ref=pairs_ref.at[chosen * mates + to],
            dst_ref=pairs_in.at[slot, at],
            send_sem=pair_send.at[slot, to],
            recv_sem=pair_recv.at[slot, at],
            device_id={"tok": half * mates + to},
            device_id_type=MESH,
        )

    def query_copy(to, at):
        return pltpu.make_async_remote_copy(
            src_ref=queries_ref.at[to],
            dst_ref=queries_in.at[at],
            send_sem=query_send.at[to],
            recv_sem=query_recv.at[at],
            device_id={"tok": to},
            device_id_type=MESH,
        )

    def out_copy(to_head, to_tok, step, from_head, from_tok):
        return pltpu.make_async_remote_copy(
            src_ref=outgoing.at[to_head, step, to_tok],
            dst_ref=arrived_ref.at[from_head, from_tok, step],
            send_sem=out_send.at[to_head, step, to_tok],
            recv_sem=out_recv.at[from_head, step, from_tok],
            device_id={"head": to_head, "tok": to_tok},
            device_id_type=MESH,
        )

    def sum_copy(part):
        return pltpu.make_async_remote_copy(
            src_ref=sums_out.at[part],
            dst_ref=sums_in.at[part],
            send_sem=sum_send.at[part],
            recv_sem=sum_recv.at[part],
            device_id={"tok": other * mates + seat},
            device_id_type=MESH,
        )

    def each_mate(core, send):
        def to_chip(step, carry):
            to = (seat // 2 + step) % near_count * 2 + core

            @pl.when(to != seat)
            def _():
                send(to)

            return carry

        lax.fori_loop(0, near_count, to_chip, 0)

    def send_pairs(slot, core):
        each_mate(core, lambda to: pair_copy(slot, to, seat).start())

    def send_queries_home(core):
        each_mate(core, lambda to: query_copy(half * mates + to, tok).start())

    def send_queries_across(core):
        def to_chip(step, carry):
            chip = other * step + half * (near_count - 1 - step)
            query_copy(other * mates + chip * 2 + core, tok).start()
            return carry

        lax.fori_loop(0, near_count, to_chip, 0)

    goes_first = seat % 2 == 0

    send_pairs(0, 0)
    send_queries_across(0)
    send_pairs(0, 1)

    lax.fori_loop(mates, shards, pack_pair, 0)

    send_pairs(1, 0)

    @pl.when(jnp.logical_not(goes_first))
    def _():
        send_queries_home(0)
        send_queries_across(1)


    block_copies = [
        pltpu.make_async_copy(pairs_ref.at[other * mates + seat], pairs_in.at[0, seat], own_sem.at[2]),
        pltpu.make_async_copy(pairs_ref.at[half * mates + seat], pairs_in.at[1, seat], own_sem.at[3]),
        pltpu.make_async_copy(queries_ref.at[tok], queries_in.at[tok], own_sem.at[4]),
    ]
    for copy in block_copies:
        copy.start()
    for copy in own_copies + block_copies:
        copy.wait()

    for slot in range(2):
        sums[...] = jnp.zeros_like(sums)

        def gather_block(step, carry):
            source = mate_from(step)

            @pl.when(step > 0)
            def _():
                pair_copy(slot, seat, source).wait_recv()

            block = pairs_in[slot, source]
            key_rows, target = block[:, :size], block[:, size:]
            first_pre = dot_nt(key_rows, weights_in[slot, 0])
            third_pre = dot_nt(key_rows, weights_in[slot, 1])
            hidden_grad = dot_nn(target, weights_in[slot, 2])
            sigmoid_first = jax.nn.sigmoid(first_pre)
            activated = first_pre * sigmoid_first
            hidden = (activated * third_pre).astype(jnp.bfloat16)
            grad_first_in = (
                hidden_grad * third_pre * sigmoid_first * (1.0 + first_pre * (1.0 - sigmoid_first))
            ).astype(jnp.bfloat16)
            grad_third_in = (hidden_grad * activated).astype(jnp.bfloat16)
            sums[0] += dot_tn(grad_first_in, key_rows)
            sums[1] += dot_tn(grad_third_in, key_rows)
            sums[2] += dot_tn(target, hidden)
            return carry

        lax.fori_loop(0, mates, gather_block, 0)
        if slot == 0:
            for part in range(3):
                total = sums[part].astype(jnp.bfloat16)
                sums_out[part] = jnp.concatenate([total[: size // 2], total[size // 2 :]], axis=1)
            sum_copy(0).start()
            sum_copy(1).start()
            sum_copy(2).start()

            @pl.when(goes_first)
            def _():
                send_queries_home(0)
                send_queries_across(1)
                send_pairs(1, 1)
                send_queries_home(1)


            @pl.when(jnp.logical_not(goes_first))
            def _():
                send_pairs(1, 1)
                send_queries_home(1)


    gate_copy = pltpu.make_async_copy(gate_ref, gate_in, own_sem.at[5])
    gate_copy.start()

    def renew(part):
        sum_copy(part).wait_recv()
        packed = sums_in[part].astype(jnp.float32)
        total = sums[part] + jnp.concatenate([packed[:, :size], packed[:, size:]], axis=0)
        renewed[part] = renormed(weights_in[1, part], total)

    gate_copy.wait()

    def open_gate(group, carry):
        lanes = pl.ds(pl.multiple_of(group * 2 * size, 2 * size), 2 * size)
        for frame in range(2 * pair_steps):
            gate = gate_in[:, frame, lanes].astype(jnp.float32)
            gate_rows[frame, :, lanes] = gate * jax.nn.sigmoid(gate)
        return carry

    lax.fori_loop(0, everyone // 2, open_gate, 0)

    renew(0)
    renew(1)

    def mix_query(step, carry):
        source = (half + step // mates) % 2 * mates + mate_from(step % mates)

        @pl.when(step > 0)
        def _():
            query_copy(tok, source).wait_recv()

        packed = queries_in[source]
        query_rows = jnp.concatenate([packed[:, :size], packed[:, size:]], axis=0)
        proj_first = dot_nt(query_rows, renewed[0])
        proj_third = dot_nt(query_rows, renewed[1])
        mixed_rows[source] = (proj_first * jax.nn.sigmoid(proj_first) * proj_third).astype(jnp.bfloat16)
        return carry

    lax.fori_loop(0, shards, mix_query, 0)
    renew(2)

    column = lax.broadcasted_iota(jnp.int32, (rows, size), 0) % width
    gain = gains_ref[pl.ds(tok, 1), :]
    height = rows // width
    edge = jnp.zeros((width, size), jnp.float32)

    def two_frames(first, second):
        mixed = jnp.concatenate([mixed_rows[first], mixed_rows[second]], axis=0)
        outputs = dot_nt(mixed, renewed[2])
        normed = outputs * lax.rsqrt(jnp.mean(outputs * outputs, axis=-1, keepdims=True) + epsilon) * gain
        normed = normed.astype(jnp.bfloat16).astype(jnp.float32)
        return jnp.concatenate([one_frame(normed[:rows]), one_frame(normed[rows:])], axis=1)

    def one_frame(middle):
        left = jnp.where(column == 0, 0.0, pltpu.roll(middle, 1, 0))
        right = jnp.where(column == width - 1, 0.0, pltpu.roll(middle, rows - 1, 0))
        bands = [
            taps_ref[3 * tap : 3 * tap + 1, :] * left
            + taps_ref[3 * tap + 1 : 3 * tap + 2, :] * middle
            + taps_ref[3 * tap + 2 : 3 * tap + 3, :] * right
            for tap in range(3)
        ]
        above = jnp.concatenate([edge, bands[0][:-width]], axis=0)
        below = jnp.concatenate([bands[2][width:], edge], axis=0)
        return above + bands[1] + below

    def frame_step(index, carry):
        to_head = (head + 1 + index // pair_steps) % head_shards
        step = index % pair_steps
        number = (to_head * pair_steps + step) * 2
        both = two_frames(inverse_ref[number], inverse_ref[number + 1])
        for lane in range(lane_groups):
            frame_pair[lane] = both[:, lane * 128 : (lane + 1) * 128]
        for x in range(width):
            for lane in range(lane_groups):
                outgoing[to_head, step, x, :, lane * 128 : (lane + 1) * 128] = frame_pair[
                    lane, pl.ds(x, height, stride=width), :
                ].astype(jnp.bfloat16)

        def send_out(offset, inner):
            to_tok = (tok + offset) % shards
            at_home = jnp.logical_and(to_head == head, offset == 0)

            @pl.when(at_home)
            def _():
                pltpu.make_async_copy(
                    outgoing.at[head, step, tok], arrived_ref.at[head, tok, step], own_out_sem.at[step]
                ).start()

            @pl.when(jnp.logical_not(at_home))
            def _():
                out_copy(to_head, to_tok, step, head, tok).start()

            return inner

        lax.fori_loop(0, shards, send_out, 0)
        return carry

    lax.fori_loop(0, head_shards * pair_steps, frame_step, 0)

    for step in range(pair_steps):
        pltpu.make_async_copy(
            outgoing.at[head, step, tok], arrived_ref.at[head, tok, step], own_out_sem.at[step]
        ).wait()

    def take_step(index, carry):
        from_head = (head + 1 + index // pair_steps) % head_shards
        step = index % pair_steps

        def take_out(offset, inner):
            from_tok = (tok - offset + shards) % shards

            @pl.when(jnp.logical_not(jnp.logical_and(from_head == head, offset == 0)))
            def _():
                out_copy(head, tok, step, from_head, from_tok).wait_recv()

            return inner

        lax.fori_loop(0, shards, take_out, 0)
        for pair in range(shards // 2):
            even = arrived_ref[from_head, 2 * pair, step].astype(jnp.float32)
            odd = arrived_ref[from_head, 2 * pair + 1, step].astype(jnp.float32)
            lanes = pl.ds(pl.multiple_of((from_head * shards + 2 * pair) * size, 2 * size), 2 * size)
            both = [
                jnp.concatenate([even[:, :size], odd[:, :size]], axis=1),
                jnp.concatenate([even[:, size:], odd[:, size:]], axis=1),
            ]
            for place in range(pair_steps):
                @pl.when(step == place)
                def _():
                    for frame in range(2):
                        gated = both[frame] * gate_rows[2 * place + frame, :, lanes]
                        gated_ref[:, 2 * place + frame, lanes] = gated.astype(jnp.bfloat16)

        return carry

    lax.fori_loop(0, head_shards * pair_steps, take_step, 0)

    for slot in range(2):
        def sent_pair(step, carry):
            pair_copy(slot, mate_at(step), seat).wait_send()
            return carry

        lax.fori_loop(1, mates, sent_pair, 0)

    def sent_query(step, carry):
        query_copy((tok + step) % shards, tok).wait_send()
        return carry

    lax.fori_loop(1, shards, sent_query, 0)
    for part in range(3):
        sum_copy(part).wait_send()
    for step in range(pair_steps):
        def sent_out(offset, carry):
            index = (head * shards + tok + offset) % everyone
            out_copy(index // shards, index % shards, step, head, tok).wait_send()
            return carry

        lax.fori_loop(1, everyone, sent_out, 0)


def by_heads(
    queries, keys, values, rates, fast_weights, norm_gain, frame_order, gate_input, conv_weights
):
    rows = queries.shape[0]
    heads = queries.shape[1] * queries.shape[2]
    size = queries.shape[3]
    shards = lax.axis_size("tok")
    head_shards = lax.axis_size("head")
    height = gate_input.shape[0]
    frames_here = gate_input.shape[1]
    pair_steps = frames_here // 2
    width = rows // height

    def by_head(values_here):
        return values_here.reshape(rows, heads, size).transpose(1, 0, 2)

    own_channel = (lax.axis_index("head") * heads + lax.axis_index("tok")) * size
    taps = lax.dynamic_slice_in_dim(conv_weights, own_channel, size, 2).reshape(9, size)
    mates = shards // 2
    in_vmem = pl.BlockSpec(memory_space=pltpu.VMEM)
    anywhere = pl.BlockSpec(memory_space=pl.ANY)
    dma = pltpu.SemaphoreType.DMA
    gated = pl.pallas_call(
        functools.partial(head_kernel, shards, head_shards, width),
        out_shape=jax.ShapeDtypeStruct((height, frames_here, head_shards * shards * size), jnp.bfloat16),
        in_specs=[pl.BlockSpec(memory_space=pltpu.SMEM)] + [in_vmem] * 4 + [anywhere, in_vmem, in_vmem, pl.BlockSpec(memory_space=pltpu.HBM)],
        out_specs=in_vmem,
        scratch_shapes=[
            pltpu.VMEM((height, frames_here, head_shards * shards * size), jnp.bfloat16),
            pltpu.VMEM((frames_here, height, head_shards * shards * size), jnp.float32),
            pltpu.VMEM((heads, rows, 2 * size), jnp.bfloat16),
            pltpu.VMEM((heads, rows // 2, 2 * size), jnp.bfloat16),
            pltpu.VMEM((2, mates, rows, 2 * size), jnp.bfloat16),
            pltpu.VMEM((shards, rows // 2, 2 * size), jnp.bfloat16),
            pltpu.VMEM((2, 3, size, size), jnp.bfloat16),
            pltpu.VMEM((3, size, size), jnp.float32),
            pltpu.VMEM((3, size // 2, 2 * size), jnp.bfloat16),
            pltpu.VMEM((3, size // 2, 2 * size), jnp.bfloat16),
            pltpu.VMEM((3, size, size), jnp.bfloat16),
            pltpu.VMEM((shards, rows, size), jnp.bfloat16),
            pltpu.VMEM((2 * size // 128, rows, 128), jnp.float32),
            pltpu.VMEM((head_shards, pair_steps, shards, height, 2 * size), jnp.bfloat16),
            pltpu.VMEM((head_shards, shards, pair_steps, height, 2 * size), jnp.bfloat16),
            pltpu.SMEM((shards,), jnp.int32),
            dma((2, mates)),
            dma((2, mates)),
            dma((shards,)),
            dma((shards,)),
            dma((3,)),
            dma((3,)),
            dma((head_shards, pair_steps, shards)),
            dma((head_shards, pair_steps, shards)),
            dma((6,)),
            dma((pair_steps,)),
        ],
        compiler_params=pltpu.CompilerParams(
            collective_id=0, has_side_effects=True, vmem_limit_bytes=44 * 1024 * 1024
        ),
    )(
        frame_order,
        by_head(queries),
        by_head(keys),
        by_head(values),
        rates.reshape(heads, rows),
        fast_weights.reshape(heads, 3, size, size),
        norm_gain.reshape(heads, size),
        taps,
        gate_input.reshape(height, frames_here, -1),
    )
    return gated.reshape(gate_input.shape)


def local(
    queries, keys, values, rates, fast_weights, norm_gain, frame_order, gate_input, conv_weights
):
    shards = lax.axis_size("tok")
    heads = queries.shape[1] * queries.shape[2]
    one_head_each = heads == shards and shards % 2 == 0
    one_column_each = gate_input.shape[2] == 1 and queries.shape[0] == gate_input.shape[0] * shards
    even = queries.shape[0] % 2 == 0 and gate_input.shape[1] % 2 == 0 and shards % 8 == 0
    even = even and 2 * queries.shape[3] % 128 == 0
    form = by_heads if one_head_each and one_column_each and even else split_rows
    return form(
        queries, keys, values, rates, fast_weights, norm_gain, frame_order, gate_input, conv_weights
    )


def solution(mesh):
    in_specs = (
        P(("groups", "tok"), "tile", "head", None),
        P(("groups", "tok"), "tile", "head", None),
        P(("groups", "tok"), "tile", "head", None),
        P("tile", "head", ("groups", "tok")),
        P("tile", "head", None, None, None),
        P("tile", "head", None),
        P("groups"),
        P(None, ("groups", "head"), "tok", "tile"),
        P(None, None, "tile"),
    )
    out_specs = P(None, ("groups", "head"), "tok", "tile")
    return jax.shard_map(local, mesh=mesh, in_specs=in_specs, out_specs=out_specs, check_vma=False)
```

```python
import functools

import jax
import jax.numpy as jnp
from jax import lax
from jax.experimental import pallas as pl
from jax.experimental.pallas import tpu as pltpu
from jax.sharding import PartitionSpec as P

MESH = pl.DeviceIdType.MESH

epsilon = 1e-06


def renormed(previous, gradient):
    before = previous.astype(jnp.float32)
    updated = before - gradient
    scale_old = jnp.sqrt(jnp.mean(before * before, axis=-1, keepdims=True) + epsilon)
    scale_new = jnp.sqrt(jnp.mean(updated * updated, axis=-1, keepdims=True) + epsilon)
    return (updated * (scale_old / scale_new)).astype(jnp.bfloat16)


def split_rows(
    queries, keys, values, rates, fast_weights, norm_gain, frame_order, gate_input, conv_weights
):
    tok_rows = queries.shape[0]
    head_count = queries.shape[1] * queries.shape[2]
    head_size = queries.shape[3]
    query_rows = queries.reshape(tok_rows, head_count, head_size)
    key_rows = keys.reshape(tok_rows, head_count, head_size)
    value_rows = values.reshape(tok_rows, head_count, head_size)
    token_rates = rates.reshape(head_count, tok_rows)
    weights = fast_weights.reshape(head_count, 3, head_size, head_size)
    head_gains = norm_gain.reshape(head_count, head_size)
    first_pre = jnp.einsum(
        "thd,hfd->htf", key_rows, weights[:, 0], preferred_element_type=jnp.float32
    )
    third_pre = jnp.einsum(
        "thd,hfd->htf", key_rows, weights[:, 1], preferred_element_type=jnp.float32
    )
    sigmoid_first = jax.nn.sigmoid(first_pre)
    activated = first_pre * sigmoid_first
    hidden = (activated * third_pre).astype(jnp.bfloat16)
    target = (-token_rates.T[:, :, None] * value_rows.astype(jnp.float32)).astype(jnp.bfloat16)
    grad_down = jnp.einsum("thd,htf->hdf", target, hidden, preferred_element_type=jnp.float32)
    hidden_grad = jnp.einsum(
        "thd,hdf->htf", target, weights[:, 2], preferred_element_type=jnp.float32
    )
    grad_first_in = (
        hidden_grad * third_pre * sigmoid_first * (1.0 + first_pre * (1.0 - sigmoid_first))
    ).astype(jnp.bfloat16)
    grad_third_in = (hidden_grad * activated).astype(jnp.bfloat16)
    grad_first = jnp.einsum(
        "htf,thd->hfd", grad_first_in, key_rows, preferred_element_type=jnp.float32
    )
    grad_third = jnp.einsum(
        "htf,thd->hfd", grad_third_in, key_rows, preferred_element_type=jnp.float32
    )
    gradients = jnp.stack([grad_first, grad_third, grad_down], axis=1)
    row_share = lax.psum_scatter(gradients, "tok", scatter_dimension=2, tiled=True)
    row_count = row_share.shape[2]
    own_rows = lax.dynamic_slice_in_dim(weights, lax.axis_index("tok") * row_count, row_count, 2)
    updated = lax.all_gather(renormed(own_rows, row_share), "tok", axis=2, tiled=True)
    proj_first = jnp.einsum(
        "thd,hfd->thf", query_rows, updated[:, 0], preferred_element_type=jnp.float32
    )
    proj_third = jnp.einsum(
        "thd,hfd->thf", query_rows, updated[:, 1], preferred_element_type=jnp.float32
    )
    mixed_hidden = (jax.nn.silu(proj_first) * proj_third).astype(jnp.bfloat16)
    outputs = jnp.einsum(
        "thf,hdf->thd", mixed_hidden, updated[:, 2], preferred_element_type=jnp.float32
    )
    normed = (
        outputs
        * lax.rsqrt(jnp.mean(outputs * outputs, axis=-1, keepdims=True) + epsilon)
        * head_gains[None]
    )
    normed = normed.astype(jnp.bfloat16)
    height = gate_input.shape[0]
    col_width = gate_input.shape[2]
    shards = lax.axis_size("tok")
    full_width = col_width * shards
    channels_here = head_count * head_size
    frame_grid = normed.reshape(height, full_width, channels_here)
    own_taps = lax.dynamic_slice_in_dim(
        conv_weights, lax.axis_index("head") * channels_here, channels_here, 2
    )
    padded = jnp.pad(frame_grid, ((1, 1), (1, 1), (0, 0)))
    local_sum = jnp.zeros((height, full_width, channels_here), jnp.float32)
    for row_tap in range(3):
        for col_tap in range(3):
            local_sum = local_sum + own_taps[row_tap, col_tap] * padded[
                row_tap : row_tap + height, col_tap : col_tap + full_width
            ].astype(jnp.float32)
    outgoing = local_sum.astype(jnp.bfloat16).reshape(height, shards, col_width, channels_here)
    arrived = lax.all_to_all(outgoing, "tok", split_axis=1, concat_axis=1, tiled=True)
    frame_count = frame_order.shape[0]
    numbers = jnp.arange(frame_count, dtype=jnp.int32)
    inverse = jnp.sum(
        jnp.where(frame_order[None, :] == numbers[:, None], numbers[None, :], 0), axis=1
    )
    ordered = jnp.take(arrived, inverse, axis=1)
    tile_block = lax.all_to_all(ordered, "head", split_axis=1, concat_axis=3, tiled=True)
    return (tile_block.astype(jnp.float32) * jax.nn.silu(gate_input.astype(jnp.float32))).astype(
        jnp.bfloat16
    )


def dot_nt(left, right):
    return lax.dot_general(left, right, (((1,), (1,)), ((), ())), preferred_element_type=jnp.float32)


def dot_nn(left, right):
    return lax.dot_general(left, right, (((1,), (0,)), ((), ())), preferred_element_type=jnp.float32)


def dot_tn(left, right):
    return lax.dot_general(left, right, (((0,), (0,)), ((), ())), preferred_element_type=jnp.float32)


def head_kernel(
    shards, head_shards, width,
    order_ref, query_rows_ref, key_rows_ref, value_rows_ref, rates_ref, weights_ref, gains_ref, taps_ref, gate_ref, gated_ref,
    gate_in, gate_rows, pairs_ref, queries_ref, pairs_in, queries_in, weights_in, sums, sums_out, sums_in, renewed, mixed_rows, frame_pair, outgoing, arrived_ref,
    inverse_ref,
    pair_send, pair_recv, query_send, query_recv, sum_send, sum_recv, out_send, out_recv, own_sem, own_out_sem,
):
    tok = lax.axis_index("tok")
    head = lax.axis_index("head")
    mates = shards // 2
    near_count = mates // 2
    half, seat = tok // mates, tok % mates
    other = 1 - half
    size = weights_ref.shape[-1]
    rows = key_rows_ref.shape[1]
    everyone = shards * head_shards
    pair_steps = outgoing.shape[1]
    lane_groups = frame_pair.shape[0]

    own_copies = [
        pltpu.make_async_copy(weights_ref.at[other * mates + seat], weights_in.at[0], own_sem.at[0]),
        pltpu.make_async_copy(weights_ref.at[half * mates + seat], weights_in.at[1], own_sem.at[1]),
    ]
    for copy in own_copies:
        copy.start()

    barrier = pltpu.get_barrier_semaphore()

    def greet(step, carry):
        index = (head * shards + tok + step) % everyone
        pl.semaphore_signal(
            barrier, inc=1, device_id={"head": index // shards, "tok": index % shards}, device_id_type=MESH
        )
        return carry

    lax.fori_loop(1, everyone, greet, 0)
    frame_count = order_ref.shape[0]
    for number in range(frame_count):
        place = jnp.int32(0)
        for shard in range(frame_count):
            place = jnp.where(order_ref[shard] == number, jnp.int32(shard), place)
        inverse_ref[number] = place

    token_rates = -rates_ref[...].T
    lane = lax.broadcasted_iota(jnp.int32, token_rates.shape, 1)

    def pack_query(index, carry):
        block = query_rows_ref[index]
        queries_ref[index] = jnp.concatenate([block[: rows // 2], block[rows // 2 :]], axis=1)
        return carry

    def pack_pair(step, carry):
        index = (other * mates + step) % shards
        rate = jnp.sum(jnp.where(lane == index, token_rates, 0.0), axis=1, keepdims=True)
        target = (rate * value_rows_ref[index].astype(jnp.float32)).astype(jnp.bfloat16)
        pairs_ref[index] = jnp.concatenate([key_rows_ref[index], target], axis=1)
        return carry

    lax.fori_loop(0, mates, pack_pair, 0)
    lax.fori_loop(0, shards, pack_query, 0)
    pl.semaphore_wait(barrier, everyone - 1)

    def mate_at(step):
        return (seat // 2 + step // 2) % near_count * 2 + (seat + step) % 2

    def mate_from(step):
        return (seat // 2 - step // 2 + near_count) % near_count * 2 + (seat + step) % 2

    def pair_copy(slot, to, at):
        chosen = other if slot == 0 else half
        return pltpu.make_async_remote_copy(
            src_ref=pairs_ref.at[chosen * mates + to],
            dst_ref=pairs_in.at[slot, at],
            send_sem=pair_send.at[slot, to],
            recv_sem=pair_recv.at[slot, at],
            device_id={"tok": half * mates + to},
            device_id_type=MESH,
        )

    def query_copy(to, at):
        return pltpu.make_async_remote_copy(
            src_ref=queries_ref.at[to],
            dst_ref=queries_in.at[at],
            send_sem=query_send.at[to],
            recv_sem=query_recv.at[at],
            device_id={"tok": to},
            device_id_type=MESH,
        )

    def out_copy(to_head, to_tok, step, from_head, from_tok):
        return pltpu.make_async_remote_copy(
            src_ref=outgoing.at[to_head, step, to_tok],
            dst_ref=arrived_ref.at[from_head, from_tok, step],
            send_sem=out_send.at[to_head, step, to_tok],
            recv_sem=out_recv.at[from_head, step, from_tok],
            device_id={"head": to_head, "tok": to_tok},
            device_id_type=MESH,
        )

    def sum_copy(part):
        return pltpu.make_async_remote_copy(
            src_ref=sums_out.at[part],
            dst_ref=sums_in.at[part],
            send_sem=sum_send.at[part],
            recv_sem=sum_recv.at[part],
            device_id={"tok": other * mates + seat},
            device_id_type=MESH,
        )

    def each_mate(core, send):
        def to_chip(step, carry):
            to = (seat // 2 + step) % near_count * 2 + core

            @pl.when(to != seat)
            def _():
                send(to)

            return carry

        lax.fori_loop(0, near_count, to_chip, 0)

    def send_pairs(slot, core):
        each_mate(core, lambda to: pair_copy(slot, to, seat).start())

    def send_queries_home(core):
        each_mate(core, lambda to: query_copy(half * mates + to, tok).start())

    def send_queries_across(core):
        def to_chip(step, carry):
            chip = other * step + half * (near_count - 1 - step)
            query_copy(other * mates + chip * 2 + core, tok).start()
            return carry

        lax.fori_loop(0, near_count, to_chip, 0)

    goes_first = seat % 2 == 0

    send_pairs(0, 0)
    send_queries_across(0)
    send_pairs(0, 1)

    lax.fori_loop(mates, shards, pack_pair, 0)

    send_pairs(1, 0)

    @pl.when(jnp.logical_not(goes_first))
    def _():
        send_queries_home(0)
        send_queries_across(1)


    block_copies = [
        pltpu.make_async_copy(pairs_ref.at[other * mates + seat], pairs_in.at[0, seat], own_sem.at[2]),
        pltpu.make_async_copy(pairs_ref.at[half * mates + seat], pairs_in.at[1, seat], own_sem.at[3]),
        pltpu.make_async_copy(queries_ref.at[tok], queries_in.at[tok], own_sem.at[4]),
    ]
    for copy in block_copies:
        copy.start()
    for copy in own_copies + block_copies:
        copy.wait()

    for slot in range(2):
        sums[...] = jnp.zeros_like(sums)

        def gather_block(step, carry):
            source = mate_from(step)

            @pl.when(step > 0)
            def _():
                pair_copy(slot, seat, source).wait_recv()

            block = pairs_in[slot, source]
            key_rows, target = block[:, :size], block[:, size:]
            first_pre = dot_nt(key_rows, weights_in[slot, 0])
            third_pre = dot_nt(key_rows, weights_in[slot, 1])
            hidden_grad = dot_nn(target, weights_in[slot, 2])
            sigmoid_first = jax.nn.sigmoid(first_pre)
            activated = first_pre * sigmoid_first
            hidden = (activated * third_pre).astype(jnp.bfloat16)
            grad_first_in = (
                hidden_grad * third_pre * sigmoid_first * (1.0 + first_pre * (1.0 - sigmoid_first))
            ).astype(jnp.bfloat16)
            grad_third_in = (hidden_grad * activated).astype(jnp.bfloat16)
            sums[0] += dot_tn(grad_first_in, key_rows)
            sums[1] += dot_tn(grad_third_in, key_rows)
            sums[2] += dot_tn(target, hidden)
            return carry

        lax.fori_loop(0, mates, gather_block, 0)
        if slot == 0:
            for part in range(3):
                total = sums[part].astype(jnp.bfloat16)
                sums_out[part] = jnp.concatenate([total[: size // 2], total[size // 2 :]], axis=1)
            sum_copy(0).start()
            sum_copy(1).start()
            sum_copy(2).start()

            @pl.when(goes_first)
            def _():
                send_queries_home(0)
                send_queries_across(1)
                send_pairs(1, 1)
                send_queries_home(1)


            @pl.when(jnp.logical_not(goes_first))
            def _():
                send_pairs(1, 1)
                send_queries_home(1)


    gate_copy = pltpu.make_async_copy(gate_ref, gate_in, own_sem.at[5])
    gate_copy.start()

    def renew(part):
        sum_copy(part).wait_recv()
        packed = sums_in[part].astype(jnp.float32)
        total = sums[part] + jnp.concatenate([packed[:, :size], packed[:, size:]], axis=0)
        renewed[part] = renormed(weights_in[1, part], total)

    gate_copy.wait()

    def open_gate(group, carry):
        lanes = pl.ds(pl.multiple_of(group * 2 * size, 2 * size), 2 * size)
        for frame in range(2 * pair_steps):
            gate = gate_in[:, frame, lanes].astype(jnp.float32)
            gate_rows[frame, :, lanes] = gate * jax.nn.sigmoid(gate)
        return carry

    lax.fori_loop(0, everyone // 2, open_gate, 0)

    renew(0)
    renew(1)

    def mix_query(step, carry):
        source = (half + step // mates) % 2 * mates + mate_from(step % mates)

        @pl.when(step > 0)
        def _():
            query_copy(tok, source).wait_recv()

        packed = queries_in[source]
        query_rows = jnp.concatenate([packed[:, :size], packed[:, size:]], axis=0)
        proj_first = dot_nt(query_rows, renewed[0])
        proj_third = dot_nt(query_rows, renewed[1])
        mixed_rows[source] = (proj_first * jax.nn.sigmoid(proj_first) * proj_third).astype(jnp.bfloat16)
        return carry

    lax.fori_loop(0, shards, mix_query, 0)
    renew(2)

    column = lax.broadcasted_iota(jnp.int32, (rows, size), 0) % width
    gain = gains_ref[pl.ds(tok, 1), :]
    height = rows // width
    edge = jnp.zeros((width, size), jnp.float32)

    def two_frames(first, second):
        mixed = jnp.concatenate([mixed_rows[first], mixed_rows[second]], axis=0)
        outputs = dot_nt(mixed, renewed[2])
        normed = outputs * lax.rsqrt(jnp.mean(outputs * outputs, axis=-1, keepdims=True) + epsilon) * gain
        normed = normed.astype(jnp.bfloat16).astype(jnp.float32)
        return jnp.concatenate([one_frame(normed[:rows]), one_frame(normed[rows:])], axis=1)

    def one_frame(middle):
        left = jnp.where(column == 0, 0.0, pltpu.roll(middle, 1, 0))
        right = jnp.where(column == width - 1, 0.0, pltpu.roll(middle, rows - 1, 0))
        bands = [
            taps_ref[3 * tap : 3 * tap + 1, :] * left
            + taps_ref[3 * tap + 1 : 3 * tap + 2, :] * middle
            + taps_ref[3 * tap + 2 : 3 * tap + 3, :] * right
            for tap in range(3)
        ]
        above = jnp.concatenate([edge, bands[0][:-width]], axis=0)
        below = jnp.concatenate([bands[2][width:], edge], axis=0)
        return above + bands[1] + below

    def frame_step(index, carry):
        to_head = (head + 1 + index // pair_steps) % head_shards
        step = index % pair_steps
        number = (to_head * pair_steps + step) * 2
        both = two_frames(inverse_ref[number], inverse_ref[number + 1])
        for lane in range(lane_groups):
            frame_pair[lane] = both[:, lane * 128 : (lane + 1) * 128]
        for x in range(width):
            for lane in range(lane_groups):
                outgoing[to_head, step, x, :, lane * 128 : (lane + 1) * 128] = frame_pair[
                    lane, pl.ds(x, height, stride=width), :
                ].astype(jnp.bfloat16)

        def send_out(offset, inner):
            to_tok = (tok + offset) % shards
            at_home = jnp.logical_and(to_head == head, offset == 0)

            @pl.when(at_home)
            def _():
                pltpu.make_async_copy(
                    outgoing.at[head, step, tok], arrived_ref.at[head, tok, step], own_out_sem.at[step]
                ).start()

            @pl.when(jnp.logical_not(at_home))
            def _():
                out_copy(to_head, to_tok, step, head, tok).start()

            return inner

        lax.fori_loop(0, shards, send_out, 0)
        return carry

    lax.fori_loop(0, head_shards * pair_steps, frame_step, 0)

    for step in range(pair_steps):
        pltpu.make_async_copy(
            outgoing.at[head, step, tok], arrived_ref.at[head, tok, step], own_out_sem.at[step]
        ).wait()

    def take_step(index, carry):
        from_head = (head + 1 + index // pair_steps) % head_shards
        step = index % pair_steps

        def take_chip(offset, inner):
            pair = (tok // 2 + offset) % (shards // 2)
            for core in range(2):
                from_tok = 2 * pair + core

                @pl.when(jnp.logical_not(jnp.logical_and(from_head == head, from_tok == tok)))
                def _():
                    out_copy(head, tok, step, from_head, from_tok).wait_recv()

            even = arrived_ref[from_head, 2 * pair, step].astype(jnp.float32)
            odd = arrived_ref[from_head, 2 * pair + 1, step].astype(jnp.float32)
            lanes = pl.ds(pl.multiple_of((from_head * shards + 2 * pair) * size, 2 * size), 2 * size)
            both = [
                jnp.concatenate([even[:, :size], odd[:, :size]], axis=1),
                jnp.concatenate([even[:, size:], odd[:, size:]], axis=1),
            ]
            for place in range(pair_steps):
                @pl.when(step == place)
                def _():
                    for frame in range(2):
                        gated = both[frame] * gate_rows[2 * place + frame, :, lanes]
                        gated_ref[:, 2 * place + frame, lanes] = gated.astype(jnp.bfloat16)

            return inner

        lax.fori_loop(0, shards // 2, take_chip, 0)
        return carry

    lax.fori_loop(0, head_shards * pair_steps, take_step, 0)

    for slot in range(2):
        def sent_pair(step, carry):
            pair_copy(slot, mate_at(step), seat).wait_send()
            return carry

        lax.fori_loop(1, mates, sent_pair, 0)

    def sent_query(step, carry):
        query_copy((tok + step) % shards, tok).wait_send()
        return carry

    lax.fori_loop(1, shards, sent_query, 0)
    for part in range(3):
        sum_copy(part).wait_send()
    for step in range(pair_steps):
        def sent_out(offset, carry):
            index = (head * shards + tok + offset) % everyone
            out_copy(index // shards, index % shards, step, head, tok).wait_send()
            return carry

        lax.fori_loop(1, everyone, sent_out, 0)


def by_heads(
    queries, keys, values, rates, fast_weights, norm_gain, frame_order, gate_input, conv_weights
):
    rows = queries.shape[0]
    heads = queries.shape[1] * queries.shape[2]
    size = queries.shape[3]
    shards = lax.axis_size("tok")
    head_shards = lax.axis_size("head")
    height = gate_input.shape[0]
    frames_here = gate_input.shape[1]
    pair_steps = frames_here // 2
    width = rows // height

    def by_head(values_here):
        return values_here.reshape(rows, heads, size).transpose(1, 0, 2)

    own_channel = (lax.axis_index("head") * heads + lax.axis_index("tok")) * size
    taps = lax.dynamic_slice_in_dim(conv_weights, own_channel, size, 2).reshape(9, size)
    mates = shards // 2
    in_vmem = pl.BlockSpec(memory_space=pltpu.VMEM)
    anywhere = pl.BlockSpec(memory_space=pl.ANY)
    dma = pltpu.SemaphoreType.DMA
    gated = pl.pallas_call(
        functools.partial(head_kernel, shards, head_shards, width),
        out_shape=jax.ShapeDtypeStruct((height, frames_here, head_shards * shards * size), jnp.bfloat16),
        in_specs=[pl.BlockSpec(memory_space=pltpu.SMEM)] + [in_vmem] * 4 + [anywhere, in_vmem, in_vmem, pl.BlockSpec(memory_space=pltpu.HBM)],
        out_specs=in_vmem,
        scratch_shapes=[
            pltpu.VMEM((height, frames_here, head_shards * shards * size), jnp.bfloat16),
            pltpu.VMEM((frames_here, height, head_shards * shards * size), jnp.float32),
            pltpu.VMEM((heads, rows, 2 * size), jnp.bfloat16),
            pltpu.VMEM((heads, rows // 2, 2 * size), jnp.bfloat16),
            pltpu.VMEM((2, mates, rows, 2 * size), jnp.bfloat16),
            pltpu.VMEM((shards, rows // 2, 2 * size), jnp.bfloat16),
            pltpu.VMEM((2, 3, size, size), jnp.bfloat16),
            pltpu.VMEM((3, size, size), jnp.float32),
            pltpu.VMEM((3, size // 2, 2 * size), jnp.bfloat16),
            pltpu.VMEM((3, size // 2, 2 * size), jnp.bfloat16),
            pltpu.VMEM((3, size, size), jnp.bfloat16),
            pltpu.VMEM((shards, rows, size), jnp.bfloat16),
            pltpu.VMEM((2 * size // 128, rows, 128), jnp.float32),
            pltpu.VMEM((head_shards, pair_steps, shards, height, 2 * size), jnp.bfloat16),
            pltpu.VMEM((head_shards, shards, pair_steps, height, 2 * size), jnp.bfloat16),
            pltpu.SMEM((shards,), jnp.int32),
            dma((2, mates)),
            dma((2, mates)),
            dma((shards,)),
            dma((shards,)),
            dma((3,)),
            dma((3,)),
            dma((head_shards, pair_steps, shards)),
            dma((head_shards, pair_steps, shards)),
            dma((6,)),
            dma((pair_steps,)),
        ],
        compiler_params=pltpu.CompilerParams(
            collective_id=0, has_side_effects=True, vmem_limit_bytes=44 * 1024 * 1024
        ),
    )(
        frame_order,
        by_head(queries),
        by_head(keys),
        by_head(values),
        rates.reshape(heads, rows),
        fast_weights.reshape(heads, 3, size, size),
        norm_gain.reshape(heads, size),
        taps,
        gate_input.reshape(height, frames_here, -1),
    )
    return gated.reshape(gate_input.shape)


def local(
    queries, keys, values, rates, fast_weights, norm_gain, frame_order, gate_input, conv_weights
):
    shards = lax.axis_size("tok")
    heads = queries.shape[1] * queries.shape[2]
    one_head_each = heads == shards and shards % 2 == 0
    one_column_each = gate_input.shape[2] == 1 and queries.shape[0] == gate_input.shape[0] * shards
    even = queries.shape[0] % 2 == 0 and gate_input.shape[1] % 2 == 0 and shards % 8 == 0
    even = even and 2 * queries.shape[3] % 128 == 0
    form = by_heads if one_head_each and one_column_each and even else split_rows
    return form(
        queries, keys, values, rates, fast_weights, norm_gain, frame_order, gate_input, conv_weights
    )


def solution(mesh):
    in_specs = (
        P(("groups", "tok"), "tile", "head", None),
        P(("groups", "tok"), "tile", "head", None),
        P(("groups", "tok"), "tile", "head", None),
        P("tile", "head", ("groups", "tok")),
        P("tile", "head", None, None, None),
        P("tile", "head", None),
        P("groups"),
        P(None, ("groups", "head"), "tok", "tile"),
        P(None, None, "tile"),
    )
    out_specs = P(None, ("groups", "head"), "tok", "tile")
    return jax.shard_map(local, mesh=mesh, in_specs=in_specs, out_specs=out_specs, check_vma=False)
```

```python
import functools

import jax
import jax.numpy as jnp
from jax import lax
from jax.experimental import pallas as pl
from jax.experimental.pallas import tpu as pltpu
from jax.sharding import PartitionSpec as P

MESH = pl.DeviceIdType.MESH

epsilon = 1e-06


def renormed(previous, gradient):
    before = previous.astype(jnp.float32)
    updated = before - gradient
    scale_old = jnp.sqrt(jnp.mean(before * before, axis=-1, keepdims=True) + epsilon)
    scale_new = jnp.sqrt(jnp.mean(updated * updated, axis=-1, keepdims=True) + epsilon)
    return (updated * (scale_old / scale_new)).astype(jnp.bfloat16)


def split_rows(
    queries, keys, values, rates, fast_weights, norm_gain, frame_order, gate_input, conv_weights
):
    tok_rows = queries.shape[0]
    head_count = queries.shape[1] * queries.shape[2]
    head_size = queries.shape[3]
    query_rows = queries.reshape(tok_rows, head_count, head_size)
    key_rows = keys.reshape(tok_rows, head_count, head_size)
    value_rows = values.reshape(tok_rows, head_count, head_size)
    token_rates = rates.reshape(head_count, tok_rows)
    weights = fast_weights.reshape(head_count, 3, head_size, head_size)
    head_gains = norm_gain.reshape(head_count, head_size)
    first_pre = jnp.einsum(
        "thd,hfd->htf", key_rows, weights[:, 0], preferred_element_type=jnp.float32
    )
    third_pre = jnp.einsum(
        "thd,hfd->htf", key_rows, weights[:, 1], preferred_element_type=jnp.float32
    )
    sigmoid_first = jax.nn.sigmoid(first_pre)
    activated = first_pre * sigmoid_first
    hidden = (activated * third_pre).astype(jnp.bfloat16)
    target = (-token_rates.T[:, :, None] * value_rows.astype(jnp.float32)).astype(jnp.bfloat16)
    grad_down = jnp.einsum("thd,htf->hdf", target, hidden, preferred_element_type=jnp.float32)
    hidden_grad = jnp.einsum(
        "thd,hdf->htf", target, weights[:, 2], preferred_element_type=jnp.float32
    )
    grad_first_in = (
        hidden_grad * third_pre * sigmoid_first * (1.0 + first_pre * (1.0 - sigmoid_first))
    ).astype(jnp.bfloat16)
    grad_third_in = (hidden_grad * activated).astype(jnp.bfloat16)
    grad_first = jnp.einsum(
        "htf,thd->hfd", grad_first_in, key_rows, preferred_element_type=jnp.float32
    )
    grad_third = jnp.einsum(
        "htf,thd->hfd", grad_third_in, key_rows, preferred_element_type=jnp.float32
    )
    gradients = jnp.stack([grad_first, grad_third, grad_down], axis=1)
    row_share = lax.psum_scatter(gradients, "tok", scatter_dimension=2, tiled=True)
    row_count = row_share.shape[2]
    own_rows = lax.dynamic_slice_in_dim(weights, lax.axis_index("tok") * row_count, row_count, 2)
    updated = lax.all_gather(renormed(own_rows, row_share), "tok", axis=2, tiled=True)
    proj_first = jnp.einsum(
        "thd,hfd->thf", query_rows, updated[:, 0], preferred_element_type=jnp.float32
    )
    proj_third = jnp.einsum(
        "thd,hfd->thf", query_rows, updated[:, 1], preferred_element_type=jnp.float32
    )
    mixed_hidden = (jax.nn.silu(proj_first) * proj_third).astype(jnp.bfloat16)
    outputs = jnp.einsum(
        "thf,hdf->thd", mixed_hidden, updated[:, 2], preferred_element_type=jnp.float32
    )
    normed = (
        outputs
        * lax.rsqrt(jnp.mean(outputs * outputs, axis=-1, keepdims=True) + epsilon)
        * head_gains[None]
    )
    normed = normed.astype(jnp.bfloat16)
    height = gate_input.shape[0]
    col_width = gate_input.shape[2]
    shards = lax.axis_size("tok")
    full_width = col_width * shards
    channels_here = head_count * head_size
    frame_grid = normed.reshape(height, full_width, channels_here)
    own_taps = lax.dynamic_slice_in_dim(
        conv_weights, lax.axis_index("head") * channels_here, channels_here, 2
    )
    padded = jnp.pad(frame_grid, ((1, 1), (1, 1), (0, 0)))
    local_sum = jnp.zeros((height, full_width, channels_here), jnp.float32)
    for row_tap in range(3):
        for col_tap in range(3):
            local_sum = local_sum + own_taps[row_tap, col_tap] * padded[
                row_tap : row_tap + height, col_tap : col_tap + full_width
            ].astype(jnp.float32)
    outgoing = local_sum.astype(jnp.bfloat16).reshape(height, shards, col_width, channels_here)
    arrived = lax.all_to_all(outgoing, "tok", split_axis=1, concat_axis=1, tiled=True)
    frame_count = frame_order.shape[0]
    numbers = jnp.arange(frame_count, dtype=jnp.int32)
    inverse = jnp.sum(
        jnp.where(frame_order[None, :] == numbers[:, None], numbers[None, :], 0), axis=1
    )
    ordered = jnp.take(arrived, inverse, axis=1)
    tile_block = lax.all_to_all(ordered, "head", split_axis=1, concat_axis=3, tiled=True)
    return (tile_block.astype(jnp.float32) * jax.nn.silu(gate_input.astype(jnp.float32))).astype(
        jnp.bfloat16
    )


def dot_nt(left, right):
    return lax.dot_general(left, right, (((1,), (1,)), ((), ())), preferred_element_type=jnp.float32)


def dot_nn(left, right):
    return lax.dot_general(left, right, (((1,), (0,)), ((), ())), preferred_element_type=jnp.float32)


def dot_tn(left, right):
    return lax.dot_general(left, right, (((0,), (0,)), ((), ())), preferred_element_type=jnp.float32)


def head_kernel(
    shards, head_shards, width,
    order_ref, query_rows_ref, key_rows_ref, value_rows_ref, rates_ref, weights_ref, gains_ref, taps_ref, gate_ref, gated_ref,
    gate_in, gate_rows, pairs_ref, queries_ref, pairs_in, queries_in, weights_in, sums, sums_out, sums_in, renewed, mixed_rows, frame_pair, outgoing, arrived_ref,
    inverse_ref,
    pair_send, pair_recv, query_send, query_recv, sum_send, sum_recv, out_send, out_recv, own_sem, own_out_sem,
):
    tok = lax.axis_index("tok")
    head = lax.axis_index("head")
    mates = shards // 2
    near_count = mates // 2
    half, seat = tok // mates, tok % mates
    other = 1 - half
    size = weights_ref.shape[-1]
    rows = key_rows_ref.shape[1]
    everyone = shards * head_shards
    pair_steps = outgoing.shape[1]
    lane_groups = frame_pair.shape[0]

    own_copies = [
        pltpu.make_async_copy(weights_ref.at[other * mates + seat], weights_in.at[0], own_sem.at[0]),
        pltpu.make_async_copy(weights_ref.at[half * mates + seat], weights_in.at[1], own_sem.at[1]),
    ]
    for copy in own_copies:
        copy.start()

    gate_copy = pltpu.make_async_copy(gate_ref, gate_in, own_sem.at[5])
    gate_copy.start()

    barrier = pltpu.get_barrier_semaphore()

    def greet(step, carry):
        index = (head * shards + tok + step) % everyone
        pl.semaphore_signal(
            barrier, inc=1, device_id={"head": index // shards, "tok": index % shards}, device_id_type=MESH
        )
        return carry

    lax.fori_loop(1, everyone, greet, 0)
    frame_count = order_ref.shape[0]
    for number in range(frame_count):
        place = jnp.int32(0)
        for shard in range(frame_count):
            place = jnp.where(order_ref[shard] == number, jnp.int32(shard), place)
        inverse_ref[number] = place

    token_rates = -rates_ref[...].T
    lane = lax.broadcasted_iota(jnp.int32, token_rates.shape, 1)

    def pack_query(index, carry):
        block = query_rows_ref[index]
        queries_ref[index] = jnp.concatenate([block[: rows // 2], block[rows // 2 :]], axis=1)
        return carry

    def pack_pair(step, carry):
        index = (other * mates + step) % shards
        rate = jnp.sum(jnp.where(lane == index, token_rates, 0.0), axis=1, keepdims=True)
        target = (rate * value_rows_ref[index].astype(jnp.float32)).astype(jnp.bfloat16)
        pairs_ref[index] = jnp.concatenate([key_rows_ref[index], target], axis=1)
        return carry

    lax.fori_loop(0, mates, pack_pair, 0)
    lax.fori_loop(0, shards, pack_query, 0)
    pl.semaphore_wait(barrier, everyone - 1)

    def mate_at(step):
        return (seat // 2 + step // 2) % near_count * 2 + (seat + step) % 2

    def mate_from(step):
        return (seat // 2 - step // 2 + near_count) % near_count * 2 + (seat + step) % 2

    def pair_copy(slot, to, at):
        chosen = other if slot == 0 else half
        return pltpu.make_async_remote_copy(
            src_ref=pairs_ref.at[chosen * mates + to],
            dst_ref=pairs_in.at[slot, at],
            send_sem=pair_send.at[slot, to],
            recv_sem=pair_recv.at[slot, at],
            device_id={"tok": half * mates + to},
            device_id_type=MESH,
        )

    def query_copy(to, at):
        return pltpu.make_async_remote_copy(
            src_ref=queries_ref.at[to],
            dst_ref=queries_in.at[at],
            send_sem=query_send.at[to],
            recv_sem=query_recv.at[at],
            device_id={"tok": to},
            device_id_type=MESH,
        )

    def out_copy(to_head, to_tok, step, from_head, from_tok):
        return pltpu.make_async_remote_copy(
            src_ref=outgoing.at[to_head, step, to_tok],
            dst_ref=arrived_ref.at[from_head, from_tok, step],
            send_sem=out_send.at[to_head, step, to_tok],
            recv_sem=out_recv.at[from_head, step, from_tok],
            device_id={"head": to_head, "tok": to_tok},
            device_id_type=MESH,
        )

    def sum_copy(part):
        return pltpu.make_async_remote_copy(
            src_ref=sums_out.at[part],
            dst_ref=sums_in.at[part],
            send_sem=sum_send.at[part],
            recv_sem=sum_recv.at[part],
            device_id={"tok": other * mates + seat},
            device_id_type=MESH,
        )

    def each_mate(core, send):
        def to_chip(step, carry):
            to = (seat // 2 + step) % near_count * 2 + core

            @pl.when(to != seat)
            def _():
                send(to)

            return carry

        lax.fori_loop(0, near_count, to_chip, 0)

    def send_pairs(slot, core):
        each_mate(core, lambda to: pair_copy(slot, to, seat).start())

    def send_queries_home(core):
        each_mate(core, lambda to: query_copy(half * mates + to, tok).start())

    def send_queries_across(core):
        def to_chip(step, carry):
            chip = other * step + half * (near_count - 1 - step)
            query_copy(other * mates + chip * 2 + core, tok).start()
            return carry

        lax.fori_loop(0, near_count, to_chip, 0)

    goes_first = seat % 2 == 0

    send_pairs(0, 0)
    send_queries_across(0)
    send_pairs(0, 1)

    lax.fori_loop(mates, shards, pack_pair, 0)

    send_pairs(1, 0)

    @pl.when(jnp.logical_not(goes_first))
    def _():
        send_queries_home(0)
        send_queries_across(1)


    block_copies = [
        pltpu.make_async_copy(pairs_ref.at[other * mates + seat], pairs_in.at[0, seat], own_sem.at[2]),
        pltpu.make_async_copy(pairs_ref.at[half * mates + seat], pairs_in.at[1, seat], own_sem.at[3]),
        pltpu.make_async_copy(queries_ref.at[tok], queries_in.at[tok], own_sem.at[4]),
    ]
    for copy in block_copies:
        copy.start()
    for copy in own_copies + block_copies:
        copy.wait()

    gate_copy.wait()

    def open_gate(group, carry):
        lanes = pl.ds(pl.multiple_of(group * 2 * size, 2 * size), 2 * size)
        for frame in range(2 * pair_steps):
            gate = gate_in[:, frame, lanes].astype(jnp.float32)
            gate_rows[frame, :, lanes] = gate * jax.nn.sigmoid(gate)
        return carry

    lax.fori_loop(0, everyone // 2, open_gate, 0)

    for slot in range(2):
        sums[...] = jnp.zeros_like(sums)

        def gather_block(step, carry):
            source = mate_from(step)

            @pl.when(step > 0)
            def _():
                pair_copy(slot, seat, source).wait_recv()

            block = pairs_in[slot, source]
            key_rows, target = block[:, :size], block[:, size:]
            first_pre = dot_nt(key_rows, weights_in[slot, 0])
            third_pre = dot_nt(key_rows, weights_in[slot, 1])
            hidden_grad = dot_nn(target, weights_in[slot, 2])
            sigmoid_first = jax.nn.sigmoid(first_pre)
            activated = first_pre * sigmoid_first
            hidden = (activated * third_pre).astype(jnp.bfloat16)
            grad_first_in = (
                hidden_grad * third_pre * sigmoid_first * (1.0 + first_pre * (1.0 - sigmoid_first))
            ).astype(jnp.bfloat16)
            grad_third_in = (hidden_grad * activated).astype(jnp.bfloat16)
            sums[0] += dot_tn(grad_first_in, key_rows)
            sums[1] += dot_tn(grad_third_in, key_rows)
            sums[2] += dot_tn(target, hidden)
            return carry

        lax.fori_loop(0, mates, gather_block, 0)
        if slot == 0:
            for part in range(3):
                total = sums[part].astype(jnp.bfloat16)
                sums_out[part] = jnp.concatenate([total[: size // 2], total[size // 2 :]], axis=1)
            sum_copy(0).start()
            sum_copy(1).start()
            sum_copy(2).start()

            @pl.when(goes_first)
            def _():
                send_queries_home(0)
                send_queries_across(1)
                send_pairs(1, 1)
                send_queries_home(1)


            @pl.when(jnp.logical_not(goes_first))
            def _():
                send_pairs(1, 1)
                send_queries_home(1)


    def renew(part):
        sum_copy(part).wait_recv()
        packed = sums_in[part].astype(jnp.float32)
        total = sums[part] + jnp.concatenate([packed[:, :size], packed[:, size:]], axis=0)
        renewed[part] = renormed(weights_in[1, part], total)

    renew(0)
    renew(1)

    def mix_query(step, carry):
        source = (half + step // mates) % 2 * mates + mate_from(step % mates)

        @pl.when(step > 0)
        def _():
            query_copy(tok, source).wait_recv()

        packed = queries_in[source]
        query_rows = jnp.concatenate([packed[:, :size], packed[:, size:]], axis=0)
        proj_first = dot_nt(query_rows, renewed[0])
        proj_third = dot_nt(query_rows, renewed[1])
        mixed_rows[source] = (proj_first * jax.nn.sigmoid(proj_first) * proj_third).astype(jnp.bfloat16)
        return carry

    lax.fori_loop(0, shards, mix_query, 0)
    renew(2)

    column = lax.broadcasted_iota(jnp.int32, (rows, size), 0) % width
    gain = gains_ref[pl.ds(tok, 1), :]
    height = rows // width
    edge = jnp.zeros((width, size), jnp.float32)

    def two_frames(first, second):
        mixed = jnp.concatenate([mixed_rows[first], mixed_rows[second]], axis=0)
        outputs = dot_nt(mixed, renewed[2])
        normed = outputs * lax.rsqrt(jnp.mean(outputs * outputs, axis=-1, keepdims=True) + epsilon) * gain
        normed = normed.astype(jnp.bfloat16).astype(jnp.float32)
        return jnp.concatenate([one_frame(normed[:rows]), one_frame(normed[rows:])], axis=1)

    def one_frame(middle):
        left = jnp.where(column == 0, 0.0, pltpu.roll(middle, 1, 0))
        right = jnp.where(column == width - 1, 0.0, pltpu.roll(middle, rows - 1, 0))
        bands = [
            taps_ref[3 * tap : 3 * tap + 1, :] * left
            + taps_ref[3 * tap + 1 : 3 * tap + 2, :] * middle
            + taps_ref[3 * tap + 2 : 3 * tap + 3, :] * right
            for tap in range(3)
        ]
        above = jnp.concatenate([edge, bands[0][:-width]], axis=0)
        below = jnp.concatenate([bands[2][width:], edge], axis=0)
        return above + bands[1] + below

    def frame_step(index, carry):
        to_head = (head + 1 + index // pair_steps) % head_shards
        step = index % pair_steps
        number = (to_head * pair_steps + step) * 2
        both = two_frames(inverse_ref[number], inverse_ref[number + 1])
        for lane in range(lane_groups):
            frame_pair[lane] = both[:, lane * 128 : (lane + 1) * 128]
        for x in range(width):
            for lane in range(lane_groups):
                outgoing[to_head, step, x, :, lane * 128 : (lane + 1) * 128] = frame_pair[
                    lane, pl.ds(x, height, stride=width), :
                ].astype(jnp.bfloat16)

        def send_out(offset, inner):
            to_tok = (tok + offset) % shards
            at_home = jnp.logical_and(to_head == head, offset == 0)

            @pl.when(at_home)
            def _():
                pltpu.make_async_copy(
                    outgoing.at[head, step, tok], arrived_ref.at[head, tok, step], own_out_sem.at[step]
                ).start()

            @pl.when(jnp.logical_not(at_home))
            def _():
                out_copy(to_head, to_tok, step, head, tok).start()

            return inner

        lax.fori_loop(0, shards, send_out, 0)
        return carry

    lax.fori_loop(0, head_shards * pair_steps, frame_step, 0)

    for step in range(pair_steps):
        pltpu.make_async_copy(
            outgoing.at[head, step, tok], arrived_ref.at[head, tok, step], own_out_sem.at[step]
        ).wait()

    def take_step(index, carry):
        from_head = (head + 1 + index // pair_steps) % head_shards
        step = index % pair_steps

        def take_chip(offset, inner):
            pair = (tok // 2 + offset) % (shards // 2)
            for core in range(2):
                from_tok = 2 * pair + core

                @pl.when(jnp.logical_not(jnp.logical_and(from_head == head, from_tok == tok)))
                def _():
                    out_copy(head, tok, step, from_head, from_tok).wait_recv()

            even = arrived_ref[from_head, 2 * pair, step].astype(jnp.float32)
            odd = arrived_ref[from_head, 2 * pair + 1, step].astype(jnp.float32)
            lanes = pl.ds(pl.multiple_of((from_head * shards + 2 * pair) * size, 2 * size), 2 * size)
            both = [
                jnp.concatenate([even[:, :size], odd[:, :size]], axis=1),
                jnp.concatenate([even[:, size:], odd[:, size:]], axis=1),
            ]
            for place in range(pair_steps):
                @pl.when(step == place)
                def _():
                    for frame in range(2):
                        gated = both[frame] * gate_rows[2 * place + frame, :, lanes]
                        gated_ref[:, 2 * place + frame, lanes] = gated.astype(jnp.bfloat16)

            return inner

        lax.fori_loop(0, shards // 2, take_chip, 0)
        return carry

    lax.fori_loop(0, head_shards * pair_steps, take_step, 0)

    for slot in range(2):
        def sent_pair(step, carry):
            pair_copy(slot, mate_at(step), seat).wait_send()
            return carry

        lax.fori_loop(1, mates, sent_pair, 0)

    def sent_query(step, carry):
        query_copy((tok + step) % shards, tok).wait_send()
        return carry

    lax.fori_loop(1, shards, sent_query, 0)
    for part in range(3):
        sum_copy(part).wait_send()
    for step in range(pair_steps):
        def sent_out(offset, carry):
            index = (head * shards + tok + offset) % everyone
            out_copy(index // shards, index % shards, step, head, tok).wait_send()
            return carry

        lax.fori_loop(1, everyone, sent_out, 0)


def by_heads(
    queries, keys, values, rates, fast_weights, norm_gain, frame_order, gate_input, conv_weights
):
    rows = queries.shape[0]
    heads = queries.shape[1] * queries.shape[2]
    size = queries.shape[3]
    shards = lax.axis_size("tok")
    head_shards = lax.axis_size("head")
    height = gate_input.shape[0]
    frames_here = gate_input.shape[1]
    pair_steps = frames_here // 2
    width = rows // height

    def by_head(values_here):
        return values_here.reshape(rows, heads, size).transpose(1, 0, 2)

    own_channel = (lax.axis_index("head") * heads + lax.axis_index("tok")) * size
    taps = lax.dynamic_slice_in_dim(conv_weights, own_channel, size, 2).reshape(9, size)
    mates = shards // 2
    in_vmem = pl.BlockSpec(memory_space=pltpu.VMEM)
    anywhere = pl.BlockSpec(memory_space=pl.ANY)
    dma = pltpu.SemaphoreType.DMA
    gated = pl.pallas_call(
        functools.partial(head_kernel, shards, head_shards, width),
        out_shape=jax.ShapeDtypeStruct((height, frames_here, head_shards * shards * size), jnp.bfloat16),
        in_specs=[pl.BlockSpec(memory_space=pltpu.SMEM)] + [in_vmem] * 4 + [anywhere, in_vmem, in_vmem, pl.BlockSpec(memory_space=pltpu.HBM)],
        out_specs=in_vmem,
        scratch_shapes=[
            pltpu.VMEM((height, frames_here, head_shards * shards * size), jnp.bfloat16),
            pltpu.VMEM((frames_here, height, head_shards * shards * size), jnp.float32),
            pltpu.VMEM((heads, rows, 2 * size), jnp.bfloat16),
            pltpu.VMEM((heads, rows // 2, 2 * size), jnp.bfloat16),
            pltpu.VMEM((2, mates, rows, 2 * size), jnp.bfloat16),
            pltpu.VMEM((shards, rows // 2, 2 * size), jnp.bfloat16),
            pltpu.VMEM((2, 3, size, size), jnp.bfloat16),
            pltpu.VMEM((3, size, size), jnp.float32),
            pltpu.VMEM((3, size // 2, 2 * size), jnp.bfloat16),
            pltpu.VMEM((3, size // 2, 2 * size), jnp.bfloat16),
            pltpu.VMEM((3, size, size), jnp.bfloat16),
            pltpu.VMEM((shards, rows, size), jnp.bfloat16),
            pltpu.VMEM((2 * size // 128, rows, 128), jnp.float32),
            pltpu.VMEM((head_shards, pair_steps, shards, height, 2 * size), jnp.bfloat16),
            pltpu.VMEM((head_shards, shards, pair_steps, height, 2 * size), jnp.bfloat16),
            pltpu.SMEM((shards,), jnp.int32),
            dma((2, mates)),
            dma((2, mates)),
            dma((shards,)),
            dma((shards,)),
            dma((3,)),
            dma((3,)),
            dma((head_shards, pair_steps, shards)),
            dma((head_shards, pair_steps, shards)),
            dma((6,)),
            dma((pair_steps,)),
        ],
        compiler_params=pltpu.CompilerParams(
            collective_id=0, has_side_effects=True, vmem_limit_bytes=44 * 1024 * 1024
        ),
    )(
        frame_order,
        by_head(queries),
        by_head(keys),
        by_head(values),
        rates.reshape(heads, rows),
        fast_weights.reshape(heads, 3, size, size),
        norm_gain.reshape(heads, size),
        taps,
        gate_input.reshape(height, frames_here, -1),
    )
    return gated.reshape(gate_input.shape)


def local(
    queries, keys, values, rates, fast_weights, norm_gain, frame_order, gate_input, conv_weights
):
    shards = lax.axis_size("tok")
    heads = queries.shape[1] * queries.shape[2]
    one_head_each = heads == shards and shards % 2 == 0
    one_column_each = gate_input.shape[2] == 1 and queries.shape[0] == gate_input.shape[0] * shards
    even = queries.shape[0] % 2 == 0 and gate_input.shape[1] % 2 == 0 and shards % 8 == 0
    even = even and 2 * queries.shape[3] % 128 == 0
    form = by_heads if one_head_each and one_column_each and even else split_rows
    return form(
        queries, keys, values, rates, fast_weights, norm_gain, frame_order, gate_input, conv_weights
    )


def solution(mesh):
    in_specs = (
        P(("groups", "tok"), "tile", "head", None),
        P(("groups", "tok"), "tile", "head", None),
        P(("groups", "tok"), "tile", "head", None),
        P("tile", "head", ("groups", "tok")),
        P("tile", "head", None, None, None),
        P("tile", "head", None),
        P("groups"),
        P(None, ("groups", "head"), "tok", "tile"),
        P(None, None, "tile"),
    )
    out_specs = P(None, ("groups", "head"), "tok", "tile")
    return jax.shard_map(local, mesh=mesh, in_specs=in_specs, out_specs=out_specs, check_vma=False)
```
